32 devices in a mesh: img: 4 (over x, core), cls: 4 (over z), tpl: 2 (over y).
Axes of the slice: x: 2, y: 2, z: 4, core: 2. Of those that a mesh axis runs over, the one named last changes fastest.
Arguments:
- images: bfloat16 [2048, 1280], P(('img', 'tpl')), may hold values from -5 to 5
- labels: int32 [2048], P(('img', 'tpl')), may hold values from 0 to 1023
- templates: bfloat16 [8, 1024, 1280], P('tpl', ('cls', 'img')), may hold values from -0.125 to 0.125
- projection: bfloat16 [1280, 1280], P('img', 'cls'), may hold values from -0.08441157 to 0.08441157
Outputs:
- grad_templates: bfloat16 [8, 1024, 1280], P('tpl', ('cls', 'img'))
- grad_projection: float32 [1280, 1280], P('img', 'cls')
The draws below stay inside these ranges and needn't reach their ends.
All inputs are finite; a program needn't handle non-finite values.
Results may differ from the reference program's by a relative error of at most 0.011.
Values may be sent and summed in bfloat16 or wider, within the bound.
No kernel may reach another device: no remote copies, remote signals or barrier semaphores. Data moves between devices by JAX's collectives and lax.ppermute only.
A program may use at most 64 MiB of HBM per device.

```python
import math
import jax
import jax.numpy as jnp
from jax import lax

D = 1280
C = 1024
TEMPLATES = 8
IMAGES = 2048


def noise_field(seed_key, shape):
    return jax.random.normal(seed_key, shape, jnp.float32)


def label_draw(key):
    drawn = jax.random.randint(jax.random.fold_in(key, 11), (IMAGES,), 0, C, dtype=jnp.int32)
    first_slot = jax.random.randint(jax.random.fold_in(key, 12), (), 0, IMAGES, dtype=jnp.int32)
    offset_slot = jax.random.randint(jax.random.fold_in(key, 13), (), 1, IMAGES, dtype=jnp.int32)
    second_slot = (first_slot + offset_slot) % IMAGES
    drawn = drawn.at[first_slot].set(C - 1)
    drawn = drawn.at[second_slot].set(0)
    return drawn.astype(jnp.int32)


def domain_basis(key):
    return jax.random.normal(jax.random.fold_in(key, 24), (8, D), jnp.float32)


def class_latent(key):
    group_count = C // 8
    single_part = noise_field(jax.random.fold_in(key, 21), (C, D))
    group_rows = noise_field(jax.random.fold_in(key, 22), (group_count, D))
    sibling_part = jnp.tile(group_rows, (8, 1))
    loading = jax.random.normal(jax.random.fold_in(key, 23), (C, 8), jnp.float32)
    basis_rows = domain_basis(key)
    domain_part = jnp.dot(loading, basis_rows, precision=lax.Precision.HIGHEST) / math.sqrt(8.0)
    return 0.632 * single_part + 0.548 * sibling_part + 0.548 * domain_part


def projection_matrix(key):
    raw_values = jax.random.normal(jax.random.fold_in(key, 31), (D, D), jnp.float32)
    return jnp.clip(raw_values, -3.0, 3.0) / math.sqrt(D)


def draw_labels(key, part):
    return label_draw(key)


def draw_projection(key, part):
    return projection_matrix(key).astype(jnp.bfloat16)


def draw_templates(key, part):
    latent = class_latent(key)
    basis_rows = domain_basis(key)
    style_coef = jax.random.normal(jax.random.fold_in(key, 52), (TEMPLATES, 8), jnp.float32)
    style_rows = jnp.dot(style_coef, basis_rows, precision=lax.Precision.HIGHEST) / math.sqrt(8.0)
    row_scale = jax.random.uniform(jax.random.fold_in(key, 53), (TEMPLATES, C, 1), jnp.float32, 0.4, 1.6)
    spread_noise = noise_field(jax.random.fold_in(key, 51), (TEMPLATES, C, D))
    mixture = 0.45 * latent[None] + 0.6 * spread_noise + 0.6 * style_rows[:, None, :]
    return jnp.clip(0.022 * row_scale * mixture, -0.12, 0.12).astype(jnp.bfloat16)


def draw_images(key, part):
    class_ids = label_draw(key)
    latent = class_latent(key)
    proj_values = projection_matrix(key)
    directions = jnp.dot(latent, proj_values, precision=lax.Precision.HIGHEST)
    directions = directions / jnp.sqrt(jnp.sum(directions * directions, axis=1, keepdims=True) + 1e-06)
    picked = jnp.take(directions, class_ids, axis=0)
    strength = jax.random.uniform(jax.random.fold_in(key, 43), (IMAGES, 1), jnp.float32, 0.15, 0.7)
    image_noise = noise_field(jax.random.fold_in(key, 41), (IMAGES, D))
    values = strength * math.sqrt(D) * picked + image_noise
    return jnp.clip(values, -5.0, 5.0).astype(jnp.bfloat16)


def setup_inputs(seed: int = 0) -> dict:
    keys = jax.random.split(jax.random.key(seed), 5)
    images = draw_images(jax.random.fold_in(keys[4], 71), 0)
    labels = draw_labels(jax.random.fold_in(keys[4], 71), 0)
    templates = draw_templates(jax.random.fold_in(keys[4], 71), 0)
    projection = draw_projection(jax.random.fold_in(keys[4], 71), 0)
    return {"images": images, "labels": labels, "templates": templates, "projection": projection}


logit_scale = 50.0
epsilon = 1e-06

def inverse_norm(values):
    return lax.rsqrt(lax.optimization_barrier(jnp.sum(values * values, axis=-1, keepdims=True)) + epsilon)

def reference(images, labels, templates, projection):
    flat_tpl = templates.reshape(TEMPLATES * C, D)
    text_z = jnp.dot(flat_tpl, projection, preferred_element_type=jnp.float32)
    text_rz = inverse_norm(text_z)
    text_u = text_z * text_rz
    mean_emb = lax.optimization_barrier(jnp.sum(text_u.reshape(TEMPLATES, C, D), axis=0)) / TEMPLATES
    mean_rn = inverse_norm(mean_emb)
    class_w = mean_emb * mean_rn
    class_b = class_w.astype(jnp.bfloat16)
    img_f = images.astype(jnp.float32)
    img_b = (img_f * inverse_norm(img_f)).astype(jnp.bfloat16)
    scores = logit_scale * jnp.dot(img_b, class_b.T, preferred_element_type=jnp.float32)
    exp_scores = jnp.exp(scores)
    totals = lax.optimization_barrier(jnp.sum(exp_scores, axis=1, keepdims=True))
    class_ids = jnp.arange(C, dtype=jnp.int32)
    one_hot = (labels[:, None] == class_ids[None, :]).astype(jnp.float32)
    grad_logit = (exp_scores / totals - one_hot).astype(jnp.bfloat16)
    class_g = logit_scale * jnp.dot(grad_logit.T, img_b, preferred_element_type=jnp.float32)
    dot_wg = lax.optimization_barrier(jnp.sum(class_w * class_g, axis=1, keepdims=True))
    grad_mean = (class_g - class_w * dot_wg) * mean_rn
    per_u = grad_mean / TEMPLATES
    u_three = text_u.reshape(TEMPLATES, C, D)
    inner_prod = lax.optimization_barrier(jnp.sum(u_three * per_u[None], axis=2, keepdims=True))
    grad_z = ((per_u[None] - u_three * inner_prod) * text_rz.reshape(TEMPLATES, C, 1)).astype(jnp.bfloat16)
    grad_flat = grad_z.reshape(TEMPLATES * C, D)
    grad_templates = jnp.dot(grad_flat, projection.T, preferred_element_type=jnp.float32).astype(jnp.bfloat16)
    grad_projection = jnp.dot(flat_tpl.T, grad_flat, preferred_element_type=jnp.float32)
    return (grad_templates.reshape(TEMPLATES, C, D), grad_projection)
```

```python
import functools

import jax
import jax.numpy as jnp
from jax import lax
from jax.experimental import pallas as pl
from jax.experimental.pallas import tpu as pltpu
from jax.sharding import PartitionSpec as P

logit_scale = 50.0
epsilon = 1e-06
MIB = 1 << 20
VM = pl.BlockSpec(memory_space=pltpu.VMEM)
HB = pl.BlockSpec(memory_space=pl.ANY)
SM = pl.BlockSpec(memory_space=pltpu.SMEM)


def inverse_norm(values):
    return lax.rsqrt(jnp.sum(values * values, axis=-1, keepdims=True) + epsilon)


def general_body(images, labels, templates, projection):
    tpl_count = templates.shape[0]
    cls_count = templates.shape[1]
    feat_width = templates.shape[2]
    tpl_total = tpl_count * lax.axis_size("tpl")
    img_count = lax.axis_size("img")
    wide_proj = lax.all_gather(projection, "cls", axis=1, tiled=True)
    full_proj = lax.all_gather(wide_proj, "img", axis=0, tiled=True)
    flat_tpl = templates.reshape(tpl_count * cls_count, feat_width)
    text_z = jnp.dot(flat_tpl, full_proj, preferred_element_type=jnp.float32)
    text_rz = inverse_norm(text_z)
    text_u = text_z * text_rz
    u_three = text_u.reshape(tpl_count, cls_count, feat_width)
    local_sum = jnp.sum(u_three, axis=0)
    mean_emb = lax.psum(local_sum, "tpl") / tpl_total
    mean_rn = inverse_norm(mean_emb)
    class_w = mean_emb * mean_rn
    class_b = class_w.astype(jnp.bfloat16)
    img_f = images.astype(jnp.float32)
    img_b = (img_f * inverse_norm(img_f)).astype(jnp.bfloat16)
    class_panel = lax.all_gather(class_b, "img", axis=0, tiled=True)
    scores = logit_scale * jnp.einsum(
        "cd,nd->cn", class_panel, img_b, preferred_element_type=jnp.float32
    )
    exp_scores = jnp.exp(scores)
    totals = lax.psum(jnp.sum(exp_scores, axis=0), "cls")
    first_id = lax.axis_index("cls") * img_count * cls_count
    class_ids = first_id + lax.broadcasted_iota(jnp.int32, (class_panel.shape[0], 1), 0)
    one_hot = (labels[None, :] == class_ids).astype(jnp.float32)
    grad_logit = (exp_scores / totals[None, :] - one_hot).astype(jnp.bfloat16)
    spread = lax.psum_scatter(
        logit_scale * jnp.dot(grad_logit, img_b, preferred_element_type=jnp.float32),
        "img",
        scatter_dimension=0,
        tiled=True,
    )
    class_g = lax.psum(spread, "tpl")
    dot_wg = jnp.sum(class_w * class_g, axis=1, keepdims=True)
    grad_mean = (class_g - class_w * dot_wg) * mean_rn
    per_u = grad_mean / tpl_total
    inner_prod = jnp.sum(u_three * per_u[None], axis=2, keepdims=True)
    grad_z = (
        (per_u[None] - u_three * inner_prod) * text_rz.reshape(tpl_count, cls_count, 1)
    ).astype(jnp.bfloat16)
    grad_flat = grad_z.reshape(tpl_count * cls_count, feat_width)
    grad_tpl = lax.dot_general(
        grad_flat, full_proj, (((1,), (1,)), ((), ())), preferred_element_type=jnp.float32
    )
    grad_templates = grad_tpl.astype(jnp.bfloat16).reshape(tpl_count, cls_count, feat_width)
    tpl_columns = lax.all_to_all(flat_tpl, "img", split_axis=1, concat_axis=0, tiled=True)
    partial_proj = lax.dot_general(
        tpl_columns,
        lax.all_gather(grad_flat, "img", axis=0, tiled=True),
        (((0,), (0,)), ((), ())),
        preferred_element_type=jnp.float32,
    )
    shared_proj = lax.psum_scatter(
        partial_proj.astype(jnp.bfloat16), "cls", scatter_dimension=1, tiled=True
    )
    grad_projection = lax.psum(shared_proj, "tpl").astype(jnp.float32)
    return (grad_templates, grad_projection)


def sds(shape, dtype):
    return jax.ShapeDtypeStruct(shape, dtype)


def swap(x, axis, mask):
    n = lax.axis_size(axis)
    return lax.ppermute(x, axis, [(i, i ^ mask) for i in range(n)])


def params(mib):
    return pltpu.CompilerParams(vmem_limit_bytes=mib * MIB)


def load_projection(me_ref, piece_refs, full_ref, sem):
    copies = []
    for k, piece in enumerate(piece_refs):
        copy = pltpu.make_async_copy(piece, full_ref.at[me_ref[0] ^ k], sem.at[k])
        copy.start()
        copies.append(copy)
    for copy in copies:
        copy.wait()


def text_kernel(n_img, n_tpl, me_ref, tpl_ref, *rest):
    pieces = rest[:n_img]
    u_ref, rz_ref, sum_ref, send_ref, full_ref, sem = rest[n_img:]
    load_projection(me_ref, pieces, full_ref, sem)
    feat = tpl_ref.shape[1]
    full = full_ref[...].reshape(feat, feat)
    z = jnp.dot(tpl_ref[...], full, preferred_element_type=jnp.float32)
    rz = inverse_norm(z)
    u = z * rz
    u_ref[...] = u
    rz_ref[...] = rz
    rows = u.shape[0] // n_tpl
    total = u[:rows]
    for t in range(1, n_tpl):
        total = total + u[t * rows : (t + 1) * rows]
    sum_ref[...] = total
    send_ref[...] = total.astype(jnp.bfloat16)


def score_kernel(tpl_total, n_piece, n_other, sum_ref, *rest):
    others = rest[:n_other]
    images = rest[n_other : n_other + n_piece]
    w_ref, rn_ref, e_ref, tot_ref = rest[n_other + n_piece :]
    mean = sum_ref[...]
    for other in others:
        mean = mean + other[...].astype(jnp.float32)
    mean = mean / tpl_total
    rn = inverse_norm(mean)
    w = mean * rn
    w_ref[...] = w
    rn_ref[...] = rn
    wb = w.astype(jnp.bfloat16)
    for k, image in enumerate(images):
        scores = logit_scale * lax.dot_general(
            wb, image[...], (((1,), (1,)), ((), ())), preferred_element_type=jnp.float32
        )
        e = jnp.exp(scores)
        e_ref[k] = e
        tot_ref[k : k + 1] = jnp.sum(e, axis=0, keepdims=True)


def grad_kernel(tpl_total, n_tpl, n_piece, n_tot, first_ref, *rest):
    tots = rest[:n_tot]
    images = rest[n_tot : n_tot + n_piece]
    e_ref, lab_ref, w_ref, rn_ref, u_ref, rz_ref, gz_ref = rest[n_tot + n_piece :]
    totals = tots[0][...]
    for other in tots[1:]:
        totals = totals + other[...]
    inv = 1.0 / totals
    rows, feat = w_ref.shape
    acc = jnp.zeros((rows, feat), jnp.float32)
    ids = first_ref[0] + lax.broadcasted_iota(jnp.int32, (rows, e_ref.shape[2]), 0)
    for k, image in enumerate(images):
        hot = (lab_ref[k : k + 1, :] == ids).astype(jnp.float32)
        gl = (e_ref[k] * inv[k : k + 1] - hot).astype(jnp.bfloat16)
        acc = acc + jnp.dot(gl, image[...], preferred_element_type=jnp.float32)
    g = logit_scale * acc
    w = w_ref[...]
    dot_wg = jnp.sum(w * g, axis=1, keepdims=True)
    per_u = (g - w * dot_wg) * rn_ref[...] / tpl_total
    for t in range(n_tpl):
        sl = slice(t * rows, (t + 1) * rows)
        u = u_ref[sl]
        inner = jnp.sum(u * per_u, axis=1, keepdims=True)
        gz_ref[sl] = ((per_u - u * inner) * rz_ref[sl]).astype(jnp.bfloat16)


def back_kernel(n_img, me_ref, gz_ref, *rest):
    pieces = rest[:n_img]
    out_ref, full_ref, sem = rest[n_img:]
    load_projection(me_ref, pieces, full_ref, sem)
    feat = gz_ref.shape[1]
    full = full_ref[...].reshape(feat, feat)
    out_ref[...] = lax.dot_general(
        gz_ref[...], full, (((1,), (1,)), ((), ())), preferred_element_type=jnp.float32
    ).astype(jnp.bfloat16)


def outer_kernel(n_img, n_cls, *rest):
    tpl = rest[:n_img]
    grads = rest[n_img : 2 * n_img]
    out_ref = rest[2 * n_img]
    acc = jnp.dot(tpl[0][...], grads[0][...], preferred_element_type=jnp.float32)
    for k in range(1, n_img):
        acc = acc + jnp.dot(tpl[k][...], grads[k][...], preferred_element_type=jnp.float32)
    width = acc.shape[1] // n_cls
    for j in range(n_cls):
        out_ref[j] = acc[:, j * width : (j + 1) * width].astype(jnp.bfloat16)


def body(images, labels, templates, projection):
    tpl_count, cls_count, feat = templates.shape
    n_tpl, n_img, n_cls = (lax.axis_size(a) for a in ("tpl", "img", "cls"))
    tpl_total = tpl_count * n_tpl
    flat_rows = tpl_count * cls_count
    f32, bf16 = jnp.float32, jnp.bfloat16
    me = lax.axis_index("img")
    me_arr = me.astype(jnp.int32).reshape(1)
    far = range(2, n_img, 2)

    img_f = images.astype(f32)
    img_b = (img_f * inverse_norm(img_f)).astype(bf16)
    pieces = {(0, 0): (img_b, labels)}

    def move(key, axis, mask, new):
        pieces[new] = tuple(swap(a, axis, mask) for a in pieces[key])

    for m in far:
        move((0, 0), "img", m, (0, m))
    for t in range(1, n_tpl):
        for m in (0, *far):
            move((0, m), "tpl", t, (t, m))
    for key in list(pieces):
        move(key, "img", 1, (key[0], key[1] ^ 1))
    order = [(t, m) for t in range(n_tpl) for m in range(n_img)]
    where = {key: k for k, key in enumerate(order)}
    image_list = [pieces[key][0] for key in order]
    label_arr = jnp.stack([pieces[key][1] for key in order])
    n_piece = len(order)
    img_rows = images.shape[0]

    wide = lax.all_gather(projection, "cls", axis=1, tiled=True)
    proj = {0: wide}
    for m in far:
        proj[m] = swap(wide, "img", m)
    for m in (0, *far):
        proj[m ^ 1] = swap(proj[m], "img", 1)
    proj_list = [proj[m] for m in range(n_img)]
    proj_rows = projection.shape[0]

    flat_tpl = templates.reshape(flat_rows, feat)
    u, rz, local_sum, send_sum = pl.pallas_call(
        functools.partial(text_kernel, n_img, tpl_count),
        out_shape=(
            sds((flat_rows, feat), f32),
            sds((flat_rows, 1), f32),
            sds((cls_count, feat), f32),
            sds((cls_count, feat), bf16),
        ),
        in_specs=[SM, VM] + [HB] * n_img,
        out_specs=(VM, VM, VM, VM),
        scratch_shapes=[
            pltpu.VMEM((n_img, proj_rows, feat), bf16),
            pltpu.SemaphoreType.DMA((n_img,)),
        ],
        compiler_params=params(24),
        name="text",
    )(me_arr, flat_tpl, *proj_list)

    others = [swap(send_sum, "tpl", t) for t in range(1, n_tpl)]
    class_w, mean_rn, e, tot = pl.pallas_call(
        functools.partial(score_kernel, tpl_total, n_piece, len(others)),
        out_shape=(
            sds((cls_count, feat), f32),
            sds((cls_count, 1), f32),
            sds((n_piece, cls_count, img_rows), f32),
            sds((n_piece, img_rows), f32),
        ),
        in_specs=[VM] * (1 + len(others) + n_piece),
        out_specs=(VM, VM, VM, VM),
        compiler_params=params(24),
        name="score",
    )(local_sum, *others, *image_list)

    total = tot
    for m in range(1, n_img):
        moved = swap(tot, "img", m)
        total = total + jnp.stack([moved[where[t, i ^ m]] for t, i in order])
    totals = [total] + [swap(total, "cls", m) for m in range(1, n_cls)]

    first_id = ((lax.axis_index("cls") * n_img + me) * cls_count).astype(jnp.int32).reshape(1)
    gz = pl.pallas_call(
        functools.partial(grad_kernel, tpl_total, tpl_count, n_piece, len(totals)),
        out_shape=sds((flat_rows, feat), bf16),
        in_specs=[SM] + [VM] * (len(totals) + n_piece + 6),
        out_specs=VM,
        compiler_params=params(24),
        name="grad",
    )(first_id, *totals, *image_list, e, label_arr, class_w, mean_rn, u, rz)

    tpl_t = flat_tpl.T.reshape(n_img, feat // n_img, flat_rows)
    cols = [
        lax.dynamic_index_in_dim(tpl_t, me ^ m, 0, keepdims=False) for m in range(n_img)
    ]
    cols = [cols[0]] + [swap(cols[m], "img", m) for m in range(1, n_img)]
    grads = {0: gz}
    for m in far:
        grads[m] = swap(gz, "img", m)
    for m in (0, *far):
        grads[m ^ 1] = swap(grads[m], "img", 1)
    blocks = pl.pallas_call(
        functools.partial(outer_kernel, n_img, n_cls),
        out_shape=sds((n_cls, feat // n_img, feat // n_cls), bf16),
        in_specs=[VM] * (2 * n_img),
        out_specs=VM,
        compiler_params=params(24),
        name="outer",
    )(*cols, *[grads[m] for m in range(n_img)])

    grad_tpl = pl.pallas_call(
        functools.partial(back_kernel, n_img),
        out_shape=sds((flat_rows, feat), bf16),
        in_specs=[SM, VM] + [HB] * n_img,
        out_specs=VM,
        scratch_shapes=[
            pltpu.VMEM((n_img, proj_rows, feat), bf16),
            pltpu.SemaphoreType.DMA((n_img,)),
        ],
        compiler_params=params(24),
        cost_estimate=pl.CostEstimate(
            flops=2 * flat_rows * feat * feat,
            bytes_accessed=2 * feat * feat + 4 * flat_rows * feat,
            transcendentals=0,
        ),
        name="back",
    )(me_arr, gz, *proj_list)

    mine = lax.axis_index("cls")
    block = lax.dynamic_index_in_dim(blocks, mine, 0, keepdims=False).astype(f32)
    for m in range(1, n_cls):
        block = block + swap(
            lax.dynamic_index_in_dim(blocks, mine ^ m, 0, keepdims=False), "cls", m
        ).astype(f32)
    partial = block.astype(bf16)
    result = partial.astype(f32)
    for t in range(1, n_tpl):
        result = result + swap(partial, "tpl", t).astype(f32)
    return grad_tpl.reshape(tpl_count, cls_count, feat), result


def solution(mesh):
    shape = mesh.shape
    in_specs = (
        P(("img", "tpl"), None),
        P(("img", "tpl")),
        P("tpl", ("cls", "img"), None),
        P("img", "cls"),
    )
    out_specs = (P("tpl", ("cls", "img"), None), P("img", "cls"))

    def step(images, labels, templates, projection):
        powers = all(shape[a] & (shape[a] - 1) == 0 for a in ("img", "cls", "tpl"))
        small = images.size * images.dtype.itemsize <= 8 * MIB
        chosen = body if powers and shape["img"] > 1 and small else general_body
        return jax.shard_map(
            chosen, mesh=mesh, in_specs=in_specs, out_specs=out_specs, check_vma=False
        )(images, labels, templates, projection)

    return step
```

```python
import functools

import jax
import jax.numpy as jnp
from jax import lax
from jax.experimental import pallas as pl
from jax.experimental.pallas import tpu as pltpu
from jax.sharding import PartitionSpec as P


logit_scale = 50.0
epsilon = 1e-06
MIB = 1 << 20
VM = pl.BlockSpec(memory_space=pltpu.VMEM)
HB = pl.BlockSpec(memory_space=pltpu.HBM)


def inverse_norm(values):
    return lax.rsqrt(jnp.sum(values * values, axis=-1, keepdims=True) + epsilon)


def general_body(images, labels, templates, projection):
    tpl_count = templates.shape[0]
    cls_count = templates.shape[1]
    feat_width = templates.shape[2]
    tpl_total = tpl_count * lax.axis_size("tpl")
    img_count = lax.axis_size("img")
    wide_proj = lax.all_gather(projection, "cls", axis=1, tiled=True)
    full_proj = lax.all_gather(wide_proj, "img", axis=0, tiled=True)
    flat_tpl = templates.reshape(tpl_count * cls_count, feat_width)
    text_z = jnp.dot(flat_tpl, full_proj, preferred_element_type=jnp.float32)
    text_rz = inverse_norm(text_z)
    text_u = text_z * text_rz
    u_three = text_u.reshape(tpl_count, cls_count, feat_width)
    local_sum = jnp.sum(u_three, axis=0)
    mean_emb = lax.psum(local_sum, "tpl") / tpl_total
    mean_rn = inverse_norm(mean_emb)
    class_w = mean_emb * mean_rn
    class_b = class_w.astype(jnp.bfloat16)
    img_f = images.astype(jnp.float32)
    img_b = (img_f * inverse_norm(img_f)).astype(jnp.bfloat16)
    class_panel = lax.all_gather(class_b, "img", axis=0, tiled=True)
    scores = logit_scale * jnp.einsum(
        "cd,nd->cn", class_panel, img_b, preferred_element_type=jnp.float32
    )
    exp_scores = jnp.exp(scores)
    totals = lax.psum(jnp.sum(exp_scores, axis=0), "cls")
    first_id = lax.axis_index("cls") * img_count * cls_count
    class_ids = first_id + lax.broadcasted_iota(jnp.int32, (class_panel.shape[0], 1), 0)
    one_hot = (labels[None, :] == class_ids).astype(jnp.float32)
    grad_logit = (exp_scores / totals[None, :] - one_hot).astype(jnp.bfloat16)
    spread = lax.psum_scatter(
        logit_scale * jnp.dot(grad_logit, img_b, preferred_element_type=jnp.float32),
        "img",
        scatter_dimension=0,
        tiled=True,
    )
    class_g = lax.psum(spread, "tpl")
    dot_wg = jnp.sum(class_w * class_g, axis=1, keepdims=True)
    grad_mean = (class_g - class_w * dot_wg) * mean_rn
    per_u = grad_mean / tpl_total
    inner_prod = jnp.sum(u_three * per_u[None], axis=2, keepdims=True)
    grad_z = (
        (per_u[None] - u_three * inner_prod) * text_rz.reshape(tpl_count, cls_count, 1)
    ).astype(jnp.bfloat16)
    grad_flat = grad_z.reshape(tpl_count * cls_count, feat_width)
    grad_tpl = lax.dot_general(
        grad_flat, full_proj, (((1,), (1,)), ((), ())), preferred_element_type=jnp.float32
    )
    grad_templates = grad_tpl.astype(jnp.bfloat16).reshape(tpl_count, cls_count, feat_width)
    tpl_columns = lax.all_to_all(flat_tpl, "img", split_axis=1, concat_axis=0, tiled=True)
    partial_proj = lax.dot_general(
        tpl_columns,
        lax.all_gather(grad_flat, "img", axis=0, tiled=True),
        (((0,), (0,)), ((), ())),
        preferred_element_type=jnp.float32,
    )
    shared_proj = lax.psum_scatter(
        partial_proj.astype(jnp.bfloat16), "cls", scatter_dimension=1, tiled=True
    )
    grad_projection = lax.psum(shared_proj, "tpl").astype(jnp.float32)
    return (grad_templates, grad_projection)


def sds(shape, dtype):
    return jax.ShapeDtypeStruct(shape, dtype)


def swap(x, axis, mask):
    n = lax.axis_size(axis)
    return lax.ppermute(x, axis, [(i, i ^ mask) for i in range(n)])


def params(mib):
    return pltpu.CompilerParams(vmem_limit_bytes=int(mib * MIB))


def start_all(pairs, sem):
    copies = [pltpu.make_async_copy(s, d, sem.at[k]) for k, (s, d) in enumerate(pairs)]
    for copy in copies:
        copy.start()
    return copies


def place(axis):
    return lax.axis_index(axis).astype(jnp.int32)


def prep_kernel(img_ref, lab_ref, proj_ref, out_ref, part_ref, buf, sem):
    share = part_ref.shape[0]
    at = pl.multiple_of(place("tpl") * share, share)
    copies = start_all([(img_ref, buf), (proj_ref.at[pl.ds(at, share)], part_ref)], sem)
    rows = img_ref.shape[0]
    lab = lab_ref[...]
    pad = jnp.zeros((14, rows), jnp.int32)
    digits = jnp.concatenate([lab // 128, lab % 128, pad], axis=0)
    out_ref[rows:] = jnp.zeros((16, out_ref.shape[1]), jnp.bfloat16)
    out_ref[rows:, :rows] = digits.astype(jnp.float32).astype(jnp.bfloat16)
    copies[0].wait()
    x = buf[...].astype(jnp.float32)
    out_ref[:rows] = (x * inverse_norm(x)).astype(jnp.bfloat16)
    copies[1].wait()


def lift_kernel(tpl_ref, out_ref, sem):
    for copy in start_all([(tpl_ref, out_ref)], sem):
        copy.wait()


def tick_kernel(lab_ref, out_ref):
    out_ref[...] = lab_ref[:, :128]


def tick(labels):
    return pl.pallas_call(
        tick_kernel,
        out_shape=sds((1, 128), jnp.int32),
        in_specs=[VM],
        out_specs=VM,
        compiler_params=params(1),
    )(labels)


def join_kernel(n_cls, *rest):
    pieces = rest[:n_cls]
    out_ref, buf, sem = rest[n_cls:]
    copies = start_all([(p, buf.at[place("cls") ^ m]) for m, p in enumerate(pieces)], sem)
    for copy in copies:
        copy.wait()
    width = buf.shape[2]
    for j in range(n_cls):
        out_ref[:, j * width : (j + 1) * width] = buf[j]


def load_projection(places, piece_refs, full_ref, sem):
    me, it = place("img"), place("tpl")
    pairs = [
        (piece, full_ref.at[me ^ m, it ^ t])
        for piece, (m, t) in zip(piece_refs, places)
    ]
    for copy in start_all(pairs, sem):
        copy.wait()


def text_kernel(places, n_tpl, tpl_ref, *rest):
    n = len(places)
    full_ref, u_ref, rz_ref, sum_ref, send_ref, sem = rest[n:]
    load_projection(places, rest[:n], full_ref, sem)
    feat = tpl_ref.shape[1]
    full = full_ref[...].reshape(feat, feat)
    z = jnp.dot(tpl_ref[...], full, preferred_element_type=jnp.float32)
    rz = inverse_norm(z)
    u = z * rz
    u_ref[...] = u
    rz_ref[...] = rz
    rows = u.shape[0] // n_tpl
    total = u[:rows]
    for t in range(1, n_tpl):
        total = total + u[t * rows : (t + 1) * rows]
    sum_ref[...] = total
    send_ref[...] = total.astype(jnp.bfloat16)


def score_kernel(tpl_total, n_piece, n_other, rows, sum_ref, *rest):
    others = rest[:n_other]
    images = rest[n_other : n_other + n_piece]
    w_ref, rn_ref, e_ref, tot_ref = rest[n_other + n_piece :]
    mean = sum_ref[...]
    for other in others:
        mean = mean + other[...].astype(jnp.float32)
    mean = mean / tpl_total
    rn = inverse_norm(mean)
    w = mean * rn
    w_ref[...] = w
    rn_ref[...] = rn
    wb = w.astype(jnp.bfloat16)
    for k in range(n_piece):
        scores = logit_scale * lax.dot_general(
            wb, images[k][:rows], (((1,), (1,)), ((), ())), preferred_element_type=jnp.float32
        )
        e = jnp.exp(scores)
        e_ref[k] = e
        tot_ref[k : k + 1] = jnp.sum(e, axis=0, keepdims=True)


def fold_totals_kernel(order, tot_ref, *rest):
    others, out_ref = rest[:-1], rest[-1]
    where = {key: k for k, key in enumerate(order)}
    for k, (t, i) in enumerate(order):
        row = tot_ref[k : k + 1]
        for m, other in enumerate(others, 1):
            j = where[t, i ^ m]
            row = row + other[j : j + 1]
        out_ref[k : k + 1] = row


def grad_kernel(tpl_total, n_tpl, n_piece, n_tot, img_rows, n_cls, *rest):
    tots = rest[:n_tot]
    images = rest[n_tot : n_tot + n_piece]
    e_ref, w_ref, rn_ref, u_ref, rz_ref = rest[n_tot + n_piece : n_tot + n_piece + 5]
    outs = rest[n_tot + n_piece + 5 :]
    gz_ref, turned = outs[0], outs[1 : 1 + n_cls]
    flip = outs[1 + n_cls]
    totals = tots[0][...]
    for other in tots[1:]:
        totals = totals + other[...]
    inv = 1.0 / totals
    rows, feat = w_ref.shape
    acc = jnp.zeros((rows, feat), jnp.float32)
    first = (place("cls") * lax.axis_size("img") + place("img")) * rows
    ids = first + lax.broadcasted_iota(jnp.int32, (rows, img_rows), 0)
    for k in range(n_piece):
        digits = images[k][img_rows:, :img_rows].astype(jnp.float32)
        lab = (digits[0:1] * 128.0 + digits[1:2]).astype(jnp.int32)
        hot = (lab == ids).astype(jnp.float32)
        gl = (e_ref[k] * inv[k : k + 1] - hot).astype(jnp.bfloat16)
        acc = acc + jnp.dot(gl, images[k][:img_rows], preferred_element_type=jnp.float32)
    g = logit_scale * acc
    w = w_ref[...]
    dot_wg = jnp.sum(w * g, axis=1, keepdims=True)
    per_u = (g - w * dot_wg) * rn_ref[...] / tpl_total
    inners = []
    for t in range(n_tpl):
        sl = slice(t * rows, (t + 1) * rows)
        u = u_ref[sl]
        inner = jnp.sum(u * per_u, axis=1, keepdims=True)
        gz_ref[sl] = ((per_u - u * inner) * rz_ref[sl]).astype(jnp.bfloat16)
        inners.append(inner)
    line = digits_row(jnp.concatenate(inners, axis=0))
    half = line.shape[1] // 2
    for a in range(feat // 128):
        sl = slice(a * 128, (a + 1) * 128)
        flip[sl] = per_u[:, sl].T
    width = feat // n_cls
    for m, out in enumerate(turned):
        at = (place("cls") ^ m) * width
        top = flip[pl.ds(pl.multiple_of(at, 8), width // 2), :]
        low = flip[pl.ds(pl.multiple_of(at + width // 2, 8), width // 2), :]
        out[: width // 2] = jnp.concatenate([top, low], axis=1).astype(jnp.bfloat16)
        out[width // 2 :] = jnp.concatenate(
            [line[:2, :half], line[:2, half:], jnp.zeros((12, half), jnp.float32)], axis=0
        ).astype(jnp.bfloat16)


def digits_row(column):
    wide = jnp.broadcast_to(column, (column.shape[0], 128)).T
    high = wide[0:1].astype(jnp.bfloat16).astype(jnp.float32)
    return jnp.concatenate([high, wide[0:1] - high], axis=0)


def turn_kernel(n_cls, u_ref, rz_ref, *rest):
    outs, flip = rest[:n_cls], rest[n_cls]
    feat = u_ref.shape[1]
    for a in range(feat // 128):
        sl = slice(a * 128, (a + 1) * 128)
        flip[sl] = u_ref[:, sl].T.astype(jnp.bfloat16)
    line = digits_row(rz_ref[...])
    line = jnp.concatenate([line, jnp.zeros((14, line.shape[1]), jnp.float32)], axis=0)
    width = feat // n_cls
    for m, out in enumerate(outs):
        at = pl.multiple_of((place("cls") ^ m) * width, width)
        out[:width] = flip[pl.ds(at, width), :]
        out[width:] = line.astype(jnp.bfloat16)


def turned_grad(unit_ref, late_ref):
    rows = unit_ref.shape[0] - 16
    unit = unit_ref[:rows].astype(jnp.float32)
    rz = unit_ref[rows:].astype(jnp.float32)
    late = late_ref[: rows // 2].astype(jnp.float32)
    tail = late_ref[rows // 2 :].astype(jnp.float32)
    span = late.shape[1] // 2
    per_u = jnp.concatenate([late[:, :span], late[:, span:]], axis=0)
    per_u = jnp.concatenate([per_u] * (unit.shape[1] // span), axis=1)
    inner = jnp.concatenate([tail[0:1] + tail[1:2], tail[2:3] + tail[3:4]], axis=1)
    return ((per_u - unit * inner) * (rz[0:1] + rz[1:2])).astype(jnp.bfloat16)


def back_kernel(gz_ref, full_ref, *rest):
    out_ref = rest[-1]
    out_ref[...] = lax.dot_general(
        gz_ref[...], full_ref[...], (((1,), (1,)), ((), ())), preferred_element_type=jnp.float32
    ).astype(jnp.bfloat16)


def outer_kernel(n_img, n_cls, held, *rest):
    units, lates = rest[:n_cls], rest[n_cls : 2 * n_cls]
    tpls = rest[2 * n_cls : -3]
    grads = [turned_grad(a, b) for a, b in zip(units, lates)]
    keep_ref, send_ref, acc_ref = rest[-3:]
    first = jnp.dot(grads[0], tpls[0][...], preferred_element_type=jnp.float32)
    plans = {}
    for z in range(n_cls):
        plans.setdefault(held(z), []).append(z)
    for plan, spots in plans.items():
        here = functools.reduce(jnp.logical_or, [place("cls") == z for z in spots])

        @pl.when(here)
        def _():
            acc = first
            for m in range(1, n_cls):
                acc = acc + jnp.dot(
                    grads[m], tpls[1 + plan[m - 1]][...], preferred_element_type=jnp.float32
                )
            acc_ref[...] = acc

    width = acc_ref.shape[1] // n_img
    for j in range(n_img):
        k = place("img") ^ j
        part = acc_ref[:, j * width : (j + 1) * width]

        @pl.when(k % 2 == 0)
        def _():
            keep_ref[k // 2] = part

        @pl.when(k % 2 == 1)
        def _():
            send_ref[k // 2] = part.astype(jnp.bfloat16)


def final_kernel(own_ref, *rest):
    total = own_ref[...]
    for other in rest[:-1]:
        total = total + other[...].astype(jnp.float32)
    rest[-1][...] = total.T


def fold_kernel(keep_ref, recv_ref, own_ref, *outs):
    own = keep_ref[0] + recv_ref[0].astype(jnp.float32)
    own_ref[...] = own
    outs[0][...] = own.astype(jnp.bfloat16)
    for k in range(1, len(outs)):
        outs[k][...] = (keep_ref[k] + recv_ref[k].astype(jnp.float32)).astype(jnp.bfloat16)


def both(x, tpl_mask, img_mask):
    if img_mask == 0:
        return swap(x, "tpl", tpl_mask)
    if tpl_mask == 0:
        return swap(x, "img", img_mask)
    n_img, n_tpl = lax.axis_size("img"), lax.axis_size("tpl")
    pairs = [
        (i * n_tpl + t, (i ^ img_mask) * n_tpl + (t ^ tpl_mask))
        for i in range(n_img)
        for t in range(n_tpl)
    ]
    return lax.ppermute(x, ("img", "tpl"), pairs)


def gather_line(x):
    n = lax.axis_size("cls")
    if n != 4:
        return (lambda z: tuple(range(n - 1))), [swap(x, "cls", m) for m in range(1, n)]
    one = swap(x, "cls", 1)
    mid = lax.ppermute(x, "cls", [(1, 2), (2, 1)])
    inner = lax.ppermute(one, "cls", [(1, 2), (2, 1)])
    outer = lax.ppermute(mid, "cls", [(1, 0), (2, 3)])
    last = lax.ppermute(inner, "cls", [(1, 0), (2, 3)])
    return (lambda z: (0, 2, 1) if z in (1, 2) else (0, 3, 4)), [one, mid, inner, outer, last]


def body(*args):
    return fast_body(*args)


def fast_body(images, labels, templates, projection):
    tpl_count, cls_count, feat = templates.shape
    n_tpl, n_img, n_cls = (lax.axis_size(a) for a in ("tpl", "img", "cls"))
    tpl_total = tpl_count * n_tpl
    flat_rows = tpl_count * cls_count
    img_rows = images.shape[0]
    proj_rows, proj_cols = projection.shape
    f32, bf16 = jnp.float32, jnp.bfloat16
    far = tuple(range(2, n_img, 2))
    tpls = tuple(range(1, n_tpl))
    label_row = labels.reshape(1, img_rows)
    ticks = [tick(label_row) for _ in range(6)]

    share = proj_rows // n_tpl
    marked, part = pl.pallas_call(
        prep_kernel,
        out_shape=(sds((img_rows + 16, feat), bf16), sds((share, proj_cols), bf16)),
        in_specs=[HB, VM, HB],
        out_specs=(VM, VM),
        scratch_shapes=[
            pltpu.VMEM((img_rows, feat), bf16),
            pltpu.SemaphoreType.DMA((2,)),
        ],
        compiler_params=params(8),
        name="prep",
    )(images, label_row, projection)
    shards = [part] + [swap(part, "cls", m) for m in range(1, n_cls)]
    images_at = {(0, 0): marked}
    for m in far:
        images_at[0, m] = swap(marked, "img", m)
    for t in tpls:
        images_at[t, 0] = swap(marked, "tpl", t)

    wide = pl.pallas_call(
        functools.partial(join_kernel, n_cls),
        out_shape=sds((share, feat), bf16),
        in_specs=[HB] * n_cls,
        out_specs=VM,
        scratch_shapes=[
            pltpu.VMEM((n_cls, share, proj_cols), bf16),
            pltpu.SemaphoreType.DMA((n_cls,)),
        ],
        compiler_params=params(4),
        name="join",
    )(*shards)
    proj_at = {(0, 0): wide}
    for m in far:
        proj_at[m, 0] = swap(wide, "img", m)
    for t in tpls:
        proj_at[0, t] = swap(wide, "tpl", t)
    for m in far:
        for t in tpls:
            proj_at[m, t] = swap(proj_at[m, 0], "tpl", t)
    for (m, t), part in list(proj_at.items()):
        proj_at[m ^ 1, t] = swap(part, "img", 1)
    places = list(proj_at)
    proj_list = list(proj_at.values())

    for m in far:
        for t in tpls:
            images_at[t, m] = swap(images_at[t, 0], "img", m)
    for (t, m), piece in list(images_at.items()):
        images_at[t, m ^ 1] = swap(piece, "img", 1)
    order = list(images_at)
    n_piece = len(order)
    image_list = list(images_at.values())

    flat_tpl = templates.reshape(flat_rows, feat)
    near_tpl = pl.pallas_call(
        lift_kernel,
        out_shape=sds((flat_rows, feat), bf16),
        in_specs=[HB],
        out_specs=VM,
        scratch_shapes=[pltpu.SemaphoreType.DMA((1,))],
        compiler_params=params(2),
        name="lift",
    )(flat_tpl)
    full, u, rz, local_sum, send_sum = pl.pallas_call(
        functools.partial(text_kernel, places, tpl_count),
        out_shape=(
            sds((n_img, n_tpl, share, feat), bf16),
            sds((flat_rows, feat), f32),
            sds((flat_rows, 1), f32),
            sds((cls_count, feat), f32),
            sds((cls_count, feat), bf16),
        ),
        in_specs=[VM] + [HB] * len(places),
        out_specs=(VM, VM, VM, VM, VM),
        scratch_shapes=[pltpu.SemaphoreType.DMA((len(places),))],
        compiler_params=params(16),
        name="text",
    )(near_tpl, *proj_list)

    held, tpl_list = gather_line(flat_tpl)
    tpl_list = [near_tpl] + tpl_list

    others = [swap(send_sum, "tpl", t) for t in tpls]
    width = feat // n_cls
    units = pl.pallas_call(
        functools.partial(turn_kernel, n_cls),
        out_shape=[sds((width + 16, flat_rows), bf16)] * n_cls,
        in_specs=[VM, VM],
        out_specs=[VM] * n_cls,
        scratch_shapes=[pltpu.VMEM((feat, flat_rows), bf16)],
        compiler_params=params(4),
        name="turn",
    )(u, rz)
    units = [units[0]] + [swap(units[m], "cls", m) for m in range(1, n_cls)]

    class_w, mean_rn, e, tot = pl.pallas_call(
        functools.partial(score_kernel, tpl_total, n_piece, len(others), img_rows),
        out_shape=(
            sds((cls_count, feat), f32),
            sds((cls_count, 1), f32),
            sds((n_piece, cls_count, img_rows), f32),
            sds((n_piece, img_rows), f32),
        ),
        in_specs=[VM] * (1 + len(others) + n_piece),
        out_specs=(VM, VM, VM, VM),
        compiler_params=params(16),
        name="score",
    )(local_sum, *others, *image_list)

    total = pl.pallas_call(
        functools.partial(fold_totals_kernel, order),
        out_shape=sds((n_piece, img_rows), f32),
        in_specs=[VM] * n_img,
        out_specs=VM,
        compiler_params=params(2),
        name="fold_totals",
    )(tot, *[swap(tot, "img", m) for m in range(1, n_img)])
    totals = [total] + [swap(total, "cls", m) for m in range(1, n_cls)]

    gz, *turned = pl.pallas_call(
        functools.partial(
            grad_kernel, tpl_total, tpl_count, n_piece, len(totals), img_rows, n_cls
        ),
        out_shape=[sds((flat_rows, feat), bf16)] + [sds((width // 2 + 16, flat_rows // 2), bf16)] * n_cls,
        in_specs=[VM] * (len(totals) + n_piece + 5),
        out_specs=[VM] * (1 + n_cls),
        scratch_shapes=[pltpu.VMEM((feat, cls_count), f32)],
        compiler_params=params(20),
        name="grad",
    )(
        *totals, *image_list, e, class_w, mean_rn, u, rz,
    )

    lates = [turned[0]] + [swap(turned[m], "cls", m) for m in range(1, n_cls)]
    grad_tpl = pl.pallas_call(
        back_kernel,
        out_shape=sds((flat_rows, feat), bf16),
        in_specs=[VM] * (2 + len(ticks)),
        out_specs=VM,
        compiler_params=params(16),
        cost_estimate=pl.CostEstimate(
            flops=2 * flat_rows * feat * feat,
            bytes_accessed=2 * feat * feat + 4 * flat_rows * feat,
            transcendentals=0,
        ),
        name="back",
    )(gz, full.reshape(feat, feat), *ticks)

    block = (width, feat // n_img)
    keep, send = pl.pallas_call(
        functools.partial(outer_kernel, n_img, n_cls, held),
        out_shape=(sds((n_img // 2, *block), f32), sds((n_img // 2, *block), bf16)),
        in_specs=[VM] * (2 * n_cls + len(tpl_list)),
        out_specs=(VM, VM),
        scratch_shapes=[pltpu.VMEM((width, feat), f32)],
        compiler_params=params(16),
        name="outer",
    )(*units, *lates, *tpl_list)
    own, own_b, *far_b = pl.pallas_call(
        fold_kernel,
        out_shape=[sds(block, f32)] + [sds(block, bf16)] * (n_img // 2),
        in_specs=[VM, VM],
        out_specs=[VM] * (1 + n_img // 2),
        compiler_params=params(8),
        name="fold",
    )(keep, swap(send, "img", 1))
    late = [
        both(([own_b] + far_b)[m // 2], t, m)
        for t in range(n_tpl)
        for m in (0, *far)
        if t or m
    ]
    result = pl.pallas_call(
        final_kernel,
        out_shape=sds((feat // n_img, width), f32),
        in_specs=[VM] * (1 + len(late)),
        out_specs=VM,
        compiler_params=params(4),
        name="final",
    )(own, *late)
    return grad_tpl.reshape(tpl_count, cls_count, feat), result


def solution(mesh):
    shape = mesh.shape
    in_specs = (
        P(("img", "tpl"), None),
        P(("img", "tpl")),
        P("tpl", ("cls", "img"), None),
        P("img", "cls"),
    )
    out_specs = (P("tpl", ("cls", "img"), None), P("img", "cls"))

    def step(images, labels, templates, projection):
        powers = all(shape[a] & (shape[a] - 1) == 0 for a in ("img", "cls", "tpl"))
        small = images.size * images.dtype.itemsize <= 8 * MIB
        chosen = body if powers and shape["img"] > 1 and small else general_body
        return jax.shard_map(
            chosen, mesh=mesh, in_specs=in_specs, out_specs=out_specs, check_vma=False
        )(images, labels, templates, projection)

    return step
```

```python
import functools

import jax
import jax.numpy as jnp
from jax import lax
from jax.experimental import pallas as pl
from jax.experimental.pallas import tpu as pltpu
from jax.sharding import PartitionSpec as P


logit_scale = 50.0
epsilon = 1e-06
MIB = 1 << 20
VM = pl.BlockSpec(memory_space=pltpu.VMEM)
HB = pl.BlockSpec(memory_space=pltpu.HBM)


def inverse_norm(values):
    return lax.rsqrt(jnp.sum(values * values, axis=-1, keepdims=True) + epsilon)


def general_body(images, labels, templates, projection):
    tpl_count = templates.shape[0]
    cls_count = templates.shape[1]
    feat_width = templates.shape[2]
    tpl_total = tpl_count * lax.axis_size("tpl")
    img_count = lax.axis_size("img")
    wide_proj = lax.all_gather(projection, "cls", axis=1, tiled=True)
    full_proj = lax.all_gather(wide_proj, "img", axis=0, tiled=True)
    flat_tpl = templates.reshape(tpl_count * cls_count, feat_width)
    text_z = jnp.dot(flat_tpl, full_proj, preferred_element_type=jnp.float32)
    text_rz = inverse_norm(text_z)
    text_u = text_z * text_rz
    u_three = text_u.reshape(tpl_count, cls_count, feat_width)
    local_sum = jnp.sum(u_three, axis=0)
    mean_emb = lax.psum(local_sum, "tpl") / tpl_total
    mean_rn = inverse_norm(mean_emb)
    class_w = mean_emb * mean_rn
    class_b = class_w.astype(jnp.bfloat16)
    img_f = images.astype(jnp.float32)
    img_b = (img_f * inverse_norm(img_f)).astype(jnp.bfloat16)
    class_panel = lax.all_gather(class_b, "img", axis=0, tiled=True)
    scores = logit_scale * jnp.einsum(
        "cd,nd->cn", class_panel, img_b, preferred_element_type=jnp.float32
    )
    exp_scores = jnp.exp(scores)
    totals = lax.psum(jnp.sum(exp_scores, axis=0), "cls")
    first_id = lax.axis_index("cls") * img_count * cls_count
    class_ids = first_id + lax.broadcasted_iota(jnp.int32, (class_panel.shape[0], 1), 0)
    one_hot = (labels[None, :] == class_ids).astype(jnp.float32)
    grad_logit = (exp_scores / totals[None, :] - one_hot).astype(jnp.bfloat16)
    spread = lax.psum_scatter(
        logit_scale * jnp.dot(grad_logit, img_b, preferred_element_type=jnp.float32),
        "img",
        scatter_dimension=0,
        tiled=True,
    )
    class_g = lax.psum(spread, "tpl")
    dot_wg = jnp.sum(class_w * class_g, axis=1, keepdims=True)
    grad_mean = (class_g - class_w * dot_wg) * mean_rn
    per_u = grad_mean / tpl_total
    inner_prod = jnp.sum(u_three * per_u[None], axis=2, keepdims=True)
    grad_z = (
        (per_u[None] - u_three * inner_prod) * text_rz.reshape(tpl_count, cls_count, 1)
    ).astype(jnp.bfloat16)
    grad_flat = grad_z.reshape(tpl_count * cls_count, feat_width)
    grad_tpl = lax.dot_general(
        grad_flat, full_proj, (((1,), (1,)), ((), ())), preferred_element_type=jnp.float32
    )
    grad_templates = grad_tpl.astype(jnp.bfloat16).reshape(tpl_count, cls_count, feat_width)
    tpl_columns = lax.all_to_all(flat_tpl, "img", split_axis=1, concat_axis=0, tiled=True)
    partial_proj = lax.dot_general(
        tpl_columns,
        lax.all_gather(grad_flat, "img", axis=0, tiled=True),
        (((0,), (0,)), ((), ())),
        preferred_element_type=jnp.float32,
    )
    shared_proj = lax.psum_scatter(
        partial_proj.astype(jnp.bfloat16), "cls", scatter_dimension=1, tiled=True
    )
    grad_projection = lax.psum(shared_proj, "tpl").astype(jnp.float32)
    return (grad_templates, grad_projection)


def sds(shape, dtype):
    return jax.ShapeDtypeStruct(shape, dtype)


def swap(x, axis, mask):
    n = lax.axis_size(axis)
    return lax.ppermute(x, axis, [(i, i ^ mask) for i in range(n)])


def params(mib):
    return pltpu.CompilerParams(vmem_limit_bytes=int(mib * MIB))


def start_all(pairs, sem):
    copies = [pltpu.make_async_copy(s, d, sem.at[k]) for k, (s, d) in enumerate(pairs)]
    for copy in copies:
        copy.start()
    return copies


def place(axis):
    return lax.axis_index(axis).astype(jnp.int32)


def prep_kernel(img_ref, lab_ref, proj_ref, out_ref, part_ref, buf, sem):
    share = part_ref.shape[0]
    at = pl.multiple_of(place("tpl") * share, share)
    copies = start_all([(img_ref, buf), (proj_ref.at[pl.ds(at, share)], part_ref)], sem)
    rows = img_ref.shape[0]
    lab = lab_ref[...]
    pad = jnp.zeros((14, rows), jnp.int32)
    digits = jnp.concatenate([lab // 128, lab % 128, pad], axis=0)
    out_ref[rows:] = jnp.zeros((16, out_ref.shape[1]), jnp.bfloat16)
    out_ref[rows:, :rows] = digits.astype(jnp.float32).astype(jnp.bfloat16)
    copies[0].wait()
    x = buf[...].astype(jnp.float32)
    out_ref[:rows] = (x * inverse_norm(x)).astype(jnp.bfloat16)
    copies[1].wait()


def lift_kernel(tpl_ref, *rest):
    outs, sem = rest[:-1], rest[-1]
    rows = outs[0].shape[0]
    pairs = [(tpl_ref.at[pl.ds(k * rows, rows)], out) for k, out in enumerate(outs)]
    for copy in start_all(pairs, sem):
        copy.wait()


def tick_kernel(lab_ref, out_ref):
    out_ref[...] = lab_ref[:, :128]


def tick(labels):
    return pl.pallas_call(
        tick_kernel,
        out_shape=sds((1, 128), jnp.int32),
        in_specs=[VM],
        out_specs=VM,
        compiler_params=params(1),
    )(labels)


def join_kernel(n_cls, *rest):
    pieces = rest[:n_cls]
    out_ref, buf, sem = rest[n_cls:]
    copies = start_all([(p, buf.at[place("cls") ^ m]) for m, p in enumerate(pieces)], sem)
    for copy in copies:
        copy.wait()
    width = buf.shape[2]
    for j in range(n_cls):
        out_ref[:, j * width : (j + 1) * width] = buf[j]


def load_projection(places, piece_refs, full_ref, sem):
    me, it = place("img"), place("tpl")
    pairs = [
        (piece, full_ref.at[me ^ m, it ^ t])
        for piece, (m, t) in zip(piece_refs, places)
    ]
    for copy in start_all(pairs, sem):
        copy.wait()


def text_kernel(places, n_tpl, n_half, *rest):
    tpls, rest = rest[:n_half], rest[n_half:]
    n = len(places)
    full_ref, u_ref, rz_ref, sum_ref, send_ref, sem = rest[n:]
    load_projection(places, rest[:n], full_ref, sem)
    feat = tpls[0].shape[1]
    full = full_ref[...].reshape(feat, feat)
    tpl = jnp.concatenate([ref[...] for ref in tpls], axis=0)
    z = jnp.dot(tpl, full, preferred_element_type=jnp.float32)
    rz = inverse_norm(z)
    u = z * rz
    u_ref[...] = u
    rz_ref[...] = rz
    rows = u.shape[0] // n_tpl
    total = u[:rows]
    for t in range(1, n_tpl):
        total = total + u[t * rows : (t + 1) * rows]
    sum_ref[...] = total
    send_ref[...] = total.astype(jnp.bfloat16)


def score_kernel(tpl_total, n_piece, n_other, rows, sum_ref, *rest):
    others = rest[:n_other]
    images = rest[n_other : n_other + n_piece]
    w_ref, rn_ref, e_ref, tot_ref = rest[n_other + n_piece :]
    mean = sum_ref[...]
    for other in others:
        mean = mean + other[...].astype(jnp.float32)
    mean = mean / tpl_total
    rn = inverse_norm(mean)
    w = mean * rn
    w_ref[...] = w
    rn_ref[...] = rn
    wb = w.astype(jnp.bfloat16)
    for k in range(n_piece):
        scores = logit_scale * lax.dot_general(
            wb, images[k][:rows], (((1,), (1,)), ((), ())), preferred_element_type=jnp.float32
        )
        e = jnp.exp(scores)
        e_ref[k] = e
        tot_ref[k : k + 1] = jnp.sum(e, axis=0, keepdims=True)


def fold_totals_kernel(order, tot_ref, *rest):
    others, out_ref = rest[:-1], rest[-1]
    where = {key: k for k, key in enumerate(order)}
    for k, (t, i) in enumerate(order):
        row = tot_ref[k : k + 1]
        for m, other in enumerate(others, 1):
            j = where[t, i ^ m]
            row = row + other[j : j + 1]
        out_ref[k : k + 1] = row


def grad_kernel(tpl_total, n_tpl, n_piece, n_tot, img_rows, n_cls, *rest):
    tots = rest[:n_tot]
    images = rest[n_tot : n_tot + n_piece]
    e_ref, w_ref, rn_ref, u_ref, rz_ref = rest[n_tot + n_piece : n_tot + n_piece + 5]
    outs = rest[n_tot + n_piece + 5 :]
    gz_ref, turned = outs[0], outs[1 : 1 + n_cls]
    flip = outs[1 + n_cls]
    totals = tots[0][...]
    for other in tots[1:]:
        totals = totals + other[...]
    inv = 1.0 / totals
    rows, feat = w_ref.shape
    acc = jnp.zeros((rows, feat), jnp.float32)
    first = (place("cls") * lax.axis_size("img") + place("img")) * rows
    ids = first + lax.broadcasted_iota(jnp.int32, (rows, img_rows), 0)
    for k in range(n_piece):
        digits = images[k][img_rows:, :img_rows].astype(jnp.float32)
        lab = (digits[0:1] * 128.0 + digits[1:2]).astype(jnp.int32)
        hot = (lab == ids).astype(jnp.float32)
        gl = (e_ref[k] * inv[k : k + 1] - hot).astype(jnp.bfloat16)
        acc = acc + jnp.dot(gl, images[k][:img_rows], preferred_element_type=jnp.float32)
    g = logit_scale * acc
    w = w_ref[...]
    dot_wg = jnp.sum(w * g, axis=1, keepdims=True)
    per_u = (g - w * dot_wg) * rn_ref[...] / tpl_total
    inners = []
    for t in range(n_tpl):
        sl = slice(t * rows, (t + 1) * rows)
        u = u_ref[sl]
        inner = jnp.sum(u * per_u, axis=1, keepdims=True)
        gz_ref[sl] = ((per_u - u * inner) * rz_ref[sl]).astype(jnp.bfloat16)
        inners.append(inner)
    line = digits_row(jnp.concatenate(inners, axis=0))
    half = line.shape[1] // 2
    for a in range(feat // 128):
        sl = slice(a * 128, (a + 1) * 128)
        flip[sl] = per_u[:, sl].T
    width = feat // n_cls
    for m, out in enumerate(turned):
        at = (place("cls") ^ m) * width
        top = flip[pl.ds(pl.multiple_of(at, 8), width // 2), :]
        low = flip[pl.ds(pl.multiple_of(at + width // 2, 8), width // 2), :]
        out[: width // 2] = jnp.concatenate([top, low], axis=1).astype(jnp.bfloat16)
        out[width // 2 :] = jnp.concatenate(
            [line[:2, :half], line[:2, half:], jnp.zeros((12, half), jnp.float32)], axis=0
        ).astype(jnp.bfloat16)


def digits_row(column):
    wide = jnp.broadcast_to(column, (column.shape[0], 128)).T
    high = wide[0:1].astype(jnp.bfloat16).astype(jnp.float32)
    return jnp.concatenate([high, wide[0:1] - high], axis=0)


def turn_kernel(n_cls, u_ref, rz_ref, *rest):
    outs, flip = rest[:n_cls], rest[n_cls]
    feat = u_ref.shape[1]
    for a in range(feat // 128):
        sl = slice(a * 128, (a + 1) * 128)
        flip[sl] = u_ref[:, sl].T.astype(jnp.bfloat16)
    line = digits_row(rz_ref[...])
    line = jnp.concatenate([line, jnp.zeros((14, line.shape[1]), jnp.float32)], axis=0)
    width = feat // n_cls
    for m, out in enumerate(outs):
        at = pl.multiple_of((place("cls") ^ m) * width, width)
        out[:width] = flip[pl.ds(at, width), :]
        out[width:] = line.astype(jnp.bfloat16)


def turned_grad(unit_ref, late_ref):
    rows = unit_ref.shape[0] - 16
    unit = unit_ref[:rows].astype(jnp.float32)
    rz = unit_ref[rows:].astype(jnp.float32)
    late = late_ref[: rows // 2].astype(jnp.float32)
    tail = late_ref[rows // 2 :].astype(jnp.float32)
    span = late.shape[1] // 2
    per_u = jnp.concatenate([late[:, :span], late[:, span:]], axis=0)
    per_u = jnp.concatenate([per_u] * (unit.shape[1] // span), axis=1)
    inner = jnp.concatenate([tail[0:1] + tail[1:2], tail[2:3] + tail[3:4]], axis=1)
    return ((per_u - unit * inner) * (rz[0:1] + rz[1:2])).astype(jnp.bfloat16)


def back_kernel(gz_ref, full_ref, *rest):
    out_ref = rest[-1]
    out_ref[...] = lax.dot_general(
        gz_ref[...], full_ref[...], (((1,), (1,)), ((), ())), preferred_element_type=jnp.float32
    ).astype(jnp.bfloat16)


def outer_kernel(n_img, n_cls, n_half, held, *rest):
    units, lates = rest[:n_cls], rest[n_cls : 2 * n_cls]
    tpls = rest[2 * n_cls : -3]
    keep_ref, send_ref, acc_ref = rest[-3:]
    grads = [turned_grad(a, b) for a, b in zip(units, lates)]

    def product(m, slot):
        parts = tpls[slot * n_half : (slot + 1) * n_half]
        tpl = jnp.concatenate([ref[...] for ref in parts], axis=0)
        return jnp.dot(grads[m], tpl, preferred_element_type=jnp.float32)

    first = product(0, 0)
    plans = {}
    for z in range(n_cls):
        plans.setdefault(held(z), []).append(z)
    for plan, spots in plans.items():
        here = functools.reduce(jnp.logical_or, [place("cls") == z for z in spots])

        @pl.when(here)
        def _():
            acc = first
            for m in range(1, n_cls):
                acc = acc + product(m, 1 + plan[m - 1])
            acc_ref[...] = acc

    width = acc_ref.shape[1] // n_img
    for j in range(n_img):
        k = place("img") ^ j
        part = acc_ref[:, j * width : (j + 1) * width]

        @pl.when(k % 2 == 0)
        def _():
            keep_ref[k // 2] = part

        @pl.when(k % 2 == 1)
        def _():
            send_ref[k // 2] = part.astype(jnp.bfloat16)


def final_kernel(own_ref, *rest):
    total = own_ref[...]
    for other in rest[:-1]:
        total = total + other[...].astype(jnp.float32)
    rest[-1][...] = total.T


def fold_kernel(keep_ref, recv_ref, own_ref, *outs):
    own = keep_ref[0] + recv_ref[0].astype(jnp.float32)
    own_ref[...] = own
    outs[0][...] = own.astype(jnp.bfloat16)
    for k in range(1, len(outs)):
        outs[k][...] = (keep_ref[k] + recv_ref[k].astype(jnp.float32)).astype(jnp.bfloat16)


def both(x, tpl_mask, img_mask):
    if img_mask == 0:
        return swap(x, "tpl", tpl_mask)
    if tpl_mask == 0:
        return swap(x, "img", img_mask)
    n_img, n_tpl = lax.axis_size("img"), lax.axis_size("tpl")
    pairs = [
        (i * n_tpl + t, (i ^ img_mask) * n_tpl + (t ^ tpl_mask))
        for i in range(n_img)
        for t in range(n_tpl)
    ]
    return lax.ppermute(x, ("img", "tpl"), pairs)


def gather_line(parts):
    n = lax.axis_size("cls")
    if n != 4:
        arrays = [[swap(x, "cls", m) for x in parts] for m in range(1, n)]
        return (lambda z: tuple(range(n - 1))), arrays
    one, mid, inner, outer, last = [], [], [], [], []
    for k, x in enumerate(parts):
        one.append(swap(x, "cls", 1))
        mid.append(lax.ppermute(x, "cls", [(1, 2), (2, 1)]))
        inner.append(lax.ppermute(one[k], "cls", [(1, 2), (2, 1)]))
        outer.append(lax.ppermute(mid[k], "cls", [(1, 0), (2, 3)]))
        last.append(lax.ppermute(inner[k], "cls", [(1, 0), (2, 3)]))
    return (lambda z: (0, 2, 1) if z in (1, 2) else (0, 3, 4)), [one, mid, inner, outer, last]


def body(*args):
    return fast_body(*args)


def fast_body(images, labels, templates, projection):
    tpl_count, cls_count, feat = templates.shape
    n_tpl, n_img, n_cls = (lax.axis_size(a) for a in ("tpl", "img", "cls"))
    tpl_total = tpl_count * n_tpl
    flat_rows = tpl_count * cls_count
    img_rows = images.shape[0]
    proj_rows, proj_cols = projection.shape
    f32, bf16 = jnp.float32, jnp.bfloat16
    far = tuple(range(2, n_img, 2))
    tpls = tuple(range(1, n_tpl))
    label_row = labels.reshape(1, img_rows)
    ticks = [tick(label_row) for _ in range(7)]

    share = proj_rows // n_tpl
    marked, part = pl.pallas_call(
        prep_kernel,
        out_shape=(sds((img_rows + 16, feat), bf16), sds((share, proj_cols), bf16)),
        in_specs=[HB, VM, HB],
        out_specs=(VM, VM),
        scratch_shapes=[
            pltpu.VMEM((img_rows, feat), bf16),
            pltpu.SemaphoreType.DMA((2,)),
        ],
        compiler_params=params(8),
        name="prep",
    )(images, label_row, projection)
    shards = [part] + [swap(part, "cls", m) for m in range(1, n_cls)]
    images_at = {(0, 0): marked}
    for m in far:
        images_at[0, m] = swap(marked, "img", m)
    for t in tpls:
        images_at[t, 0] = swap(marked, "tpl", t)

    wide = pl.pallas_call(
        functools.partial(join_kernel, n_cls),
        out_shape=sds((share, feat), bf16),
        in_specs=[HB] * n_cls,
        out_specs=VM,
        scratch_shapes=[
            pltpu.VMEM((n_cls, share, proj_cols), bf16),
            pltpu.SemaphoreType.DMA((n_cls,)),
        ],
        compiler_params=params(4),
        name="join",
    )(*shards)
    proj_at = {(0, 0): wide}
    for m in far:
        proj_at[m, 0] = swap(wide, "img", m)
    for t in tpls:
        proj_at[0, t] = swap(wide, "tpl", t)
    for m in far:
        for t in tpls:
            proj_at[m, t] = swap(proj_at[m, 0], "tpl", t)
    for (m, t), part in list(proj_at.items()):
        proj_at[m ^ 1, t] = swap(part, "img", 1)
    places = list(proj_at)
    proj_list = list(proj_at.values())

    for m in far:
        for t in tpls:
            images_at[t, m] = swap(images_at[t, 0], "img", m)
    for (t, m), piece in list(images_at.items()):
        images_at[t, m ^ 1] = swap(piece, "img", 1)
    order = list(images_at)
    n_piece = len(order)
    image_list = list(images_at.values())

    flat_tpl = templates.reshape(flat_rows, feat)
    near_tpl = pl.pallas_call(
        lift_kernel,
        out_shape=[sds((flat_rows // 2, feat), bf16)] * 2,
        in_specs=[HB],
        out_specs=[VM] * 2,
        scratch_shapes=[pltpu.SemaphoreType.DMA((2,))],
        compiler_params=params(2),
        name="lift",
    )(flat_tpl)
    full, u, rz, local_sum, send_sum = pl.pallas_call(
        functools.partial(text_kernel, places, tpl_count, len(near_tpl)),
        out_shape=(
            sds((n_img, n_tpl, share, feat), bf16),
            sds((flat_rows, feat), f32),
            sds((flat_rows, 1), f32),
            sds((cls_count, feat), f32),
            sds((cls_count, feat), bf16),
        ),
        in_specs=[VM] * len(near_tpl) + [HB] * len(places),
        out_specs=(VM, VM, VM, VM, VM),
        scratch_shapes=[pltpu.SemaphoreType.DMA((len(places),))],
        compiler_params=params(16),
        name="text",
    )(*near_tpl, *proj_list)

    held, tpl_parts = gather_line(near_tpl)
    tpl_list = [x for parts in [near_tpl] + tpl_parts for x in parts]

    others = [swap(send_sum, "tpl", t) for t in tpls]
    width = feat // n_cls
    units = pl.pallas_call(
        functools.partial(turn_kernel, n_cls),
        out_shape=[sds((width + 16, flat_rows), bf16)] * n_cls,
        in_specs=[VM, VM],
        out_specs=[VM] * n_cls,
        scratch_shapes=[pltpu.VMEM((feat, flat_rows), bf16)],
        compiler_params=params(4),
        name="turn",
    )(u, rz)
    units = [units[0]] + [swap(units[m], "cls", m) for m in range(1, n_cls)]

    class_w, mean_rn, e, tot = pl.pallas_call(
        functools.partial(score_kernel, tpl_total, n_piece, len(others), img_rows),
        out_shape=(
            sds((cls_count, feat), f32),
            sds((cls_count, 1), f32),
            sds((n_piece, cls_count, img_rows), f32),
            sds((n_piece, img_rows), f32),
        ),
        in_specs=[VM] * (1 + len(others) + n_piece),
        out_specs=(VM, VM, VM, VM),
        compiler_params=params(16),
        name="score",
    )(local_sum, *others, *image_list)

    total = pl.pallas_call(
        functools.partial(fold_totals_kernel, order),
        out_shape=sds((n_piece, img_rows), f32),
        in_specs=[VM] * n_img,
        out_specs=VM,
        compiler_params=params(2),
        name="fold_totals",
    )(tot, *[swap(tot, "img", m) for m in range(1, n_img)])
    totals = [total] + [swap(total, "cls", m) for m in range(1, n_cls)]

    gz, *turned = pl.pallas_call(
        functools.partial(
            grad_kernel, tpl_total, tpl_count, n_piece, len(totals), img_rows, n_cls
        ),
        out_shape=[sds((flat_rows, feat), bf16)] + [sds((width // 2 + 16, flat_rows // 2), bf16)] * n_cls,
        in_specs=[VM] * (len(totals) + n_piece + 5),
        out_specs=[VM] * (1 + n_cls),
        scratch_shapes=[pltpu.VMEM((feat, cls_count), f32)],
        compiler_params=params(20),
        name="grad",
    )(
        *totals, *image_list, e, class_w, mean_rn, u, rz,
    )

    lates = [turned[0]] + [swap(turned[m], "cls", m) for m in range(1, n_cls)]
    grad_tpl = pl.pallas_call(
        back_kernel,
        out_shape=sds((flat_rows, feat), bf16),
        in_specs=[VM] * (2 + len(ticks)),
        out_specs=VM,
        compiler_params=params(16),
        cost_estimate=pl.CostEstimate(
            flops=2 * flat_rows * feat * feat,
            bytes_accessed=2 * feat * feat + 4 * flat_rows * feat,
            transcendentals=0,
        ),
        name="back",
    )(gz, full.reshape(feat, feat), *ticks)

    block = (width, feat // n_img)
    keep, send = pl.pallas_call(
        functools.partial(outer_kernel, n_img, n_cls, len(near_tpl), held),
        out_shape=(sds((n_img // 2, *block), f32), sds((n_img // 2, *block), bf16)),
        in_specs=[VM] * (2 * n_cls + len(tpl_list)),
        out_specs=(VM, VM),
        scratch_shapes=[pltpu.VMEM((width, feat), f32)],
        compiler_params=params(16),
        name="outer",
    )(*units, *lates, *tpl_list)
    own, own_b, *far_b = pl.pallas_call(
        fold_kernel,
        out_shape=[sds(block, f32)] + [sds(block, bf16)] * (n_img // 2),
        in_specs=[VM, VM],
        out_specs=[VM] * (1 + n_img // 2),
        compiler_params=params(8),
        name="fold",
    )(keep, swap(send, "img", 1))
    late = [
        both(([own_b] + far_b)[m // 2], t, m)
        for t in range(n_tpl)
        for m in (0, *far)
        if t or m
    ]
    result = pl.pallas_call(
        final_kernel,
        out_shape=sds((feat // n_img, width), f32),
        in_specs=[VM] * (1 + len(late)),
        out_specs=VM,
        compiler_params=params(4),
        name="final",
    )(own, *late)
    return grad_tpl.reshape(tpl_count, cls_count, feat), result


def solution(mesh):
    shape = mesh.shape
    in_specs = (
        P(("img", "tpl"), None),
        P(("img", "tpl")),
        P("tpl", ("cls", "img"), None),
        P("img", "cls"),
    )
    out_specs = (P("tpl", ("cls", "img"), None), P("img", "cls"))

    def step(images, labels, templates, projection):
        powers = all(shape[a] & (shape[a] - 1) == 0 for a in ("img", "cls", "tpl"))
        small = images.size * images.dtype.itemsize <= 8 * MIB
        chosen = body if powers and shape["img"] > 1 and small else general_body
        return jax.shard_map(
            chosen, mesh=mesh, in_specs=in_specs, out_specs=out_specs, check_vma=False
        )(images, labels, templates, projection)

    return step
```

```python
import functools

import jax
import jax.numpy as jnp
from jax import lax
from jax.experimental import pallas as pl
from jax.experimental.pallas import tpu as pltpu
from jax.sharding import PartitionSpec as P


logit_scale = 50.0
epsilon = 1e-06
MIB = 1 << 20
VM = pl.BlockSpec(memory_space=pltpu.VMEM)
HB = pl.BlockSpec(memory_space=pltpu.HBM)


def inverse_norm(values):
    return lax.rsqrt(jnp.sum(values * values, axis=-1, keepdims=True) + epsilon)


def general_body(images, labels, templates, projection):
    tpl_count = templates.shape[0]
    cls_count = templates.shape[1]
    feat_width = templates.shape[2]
    tpl_total = tpl_count * lax.axis_size("tpl")
    img_count = lax.axis_size("img")
    wide_proj = lax.all_gather(projection, "cls", axis=1, tiled=True)
    full_proj = lax.all_gather(wide_proj, "img", axis=0, tiled=True)
    flat_tpl = templates.reshape(tpl_count * cls_count, feat_width)
    text_z = jnp.dot(flat_tpl, full_proj, preferred_element_type=jnp.float32)
    text_rz = inverse_norm(text_z)
    text_u = text_z * text_rz
    u_three = text_u.reshape(tpl_count, cls_count, feat_width)
    local_sum = jnp.sum(u_three, axis=0)
    mean_emb = lax.psum(local_sum, "tpl") / tpl_total
    mean_rn = inverse_norm(mean_emb)
    class_w = mean_emb * mean_rn
    class_b = class_w.astype(jnp.bfloat16)
    img_f = images.astype(jnp.float32)
    img_b = (img_f * inverse_norm(img_f)).astype(jnp.bfloat16)
    class_panel = lax.all_gather(class_b, "img", axis=0, tiled=True)
    scores = logit_scale * jnp.einsum(
        "cd,nd->cn", class_panel, img_b, preferred_element_type=jnp.float32
    )
    exp_scores = jnp.exp(scores)
    totals = lax.psum(jnp.sum(exp_scores, axis=0), "cls")
    first_id = lax.axis_index("cls") * img_count * cls_count
    class_ids = first_id + lax.broadcasted_iota(jnp.int32, (class_panel.shape[0], 1), 0)
    one_hot = (labels[None, :] == class_ids).astype(jnp.float32)
    grad_logit = (exp_scores / totals[None, :] - one_hot).astype(jnp.bfloat16)
    spread = lax.psum_scatter(
        logit_scale * jnp.dot(grad_logit, img_b, preferred_element_type=jnp.float32),
        "img",
        scatter_dimension=0,
        tiled=True,
    )
    class_g = lax.psum(spread, "tpl")
    dot_wg = jnp.sum(class_w * class_g, axis=1, keepdims=True)
    grad_mean = (class_g - class_w * dot_wg) * mean_rn
    per_u = grad_mean / tpl_total
    inner_prod = jnp.sum(u_three * per_u[None], axis=2, keepdims=True)
    grad_z = (
        (per_u[None] - u_three * inner_prod) * text_rz.reshape(tpl_count, cls_count, 1)
    ).astype(jnp.bfloat16)
    grad_flat = grad_z.reshape(tpl_count * cls_count, feat_width)
    grad_tpl = lax.dot_general(
        grad_flat, full_proj, (((1,), (1,)), ((), ())), preferred_element_type=jnp.float32
    )
    grad_templates = grad_tpl.astype(jnp.bfloat16).reshape(tpl_count, cls_count, feat_width)
    tpl_columns = lax.all_to_all(flat_tpl, "img", split_axis=1, concat_axis=0, tiled=True)
    partial_proj = lax.dot_general(
        tpl_columns,
        lax.all_gather(grad_flat, "img", axis=0, tiled=True),
        (((0,), (0,)), ((), ())),
        preferred_element_type=jnp.float32,
    )
    shared_proj = lax.psum_scatter(
        partial_proj.astype(jnp.bfloat16), "cls", scatter_dimension=1, tiled=True
    )
    grad_projection = lax.psum(shared_proj, "tpl").astype(jnp.float32)
    return (grad_templates, grad_projection)


def sds(shape, dtype):
    return jax.ShapeDtypeStruct(shape, dtype)


def swap(x, axis, mask):
    n = lax.axis_size(axis)
    return lax.ppermute(x, axis, [(i, i ^ mask) for i in range(n)])


def params(mib):
    return pltpu.CompilerParams(vmem_limit_bytes=int(mib * MIB))


def start_all(pairs, sem):
    copies = [pltpu.make_async_copy(s, d, sem.at[k]) for k, (s, d) in enumerate(pairs)]
    for copy in copies:
        copy.start()
    return copies


def packing(rows, cols):
    lanes, rest = cols // 128 * 128, cols % 128
    if rest and lanes % rest == 0 and rows % (lanes // rest * 8) == 0:
        return lanes, rest, lanes // rest
    return cols, 0, 0


def packed_shape(rows, cols):
    lanes, rest, pieces = packing(rows, cols)
    return (rows + rows // pieces, lanes) if rest else (rows, cols)


def pack(x):
    rows, cols = x.shape
    lanes, rest, pieces = packing(rows, cols)
    if not rest:
        return x
    step = rows // pieces
    side = [x[q * step : (q + 1) * step, lanes:] for q in range(pieces)]
    return jnp.concatenate([x[:, :lanes], jnp.concatenate(side, axis=1)], axis=0)


def unpack(x, rows, cols):
    _, rest, pieces = packing(rows, cols)
    if not rest:
        return x
    side = [x[rows:, q * rest : (q + 1) * rest] for q in range(pieces)]
    return jnp.concatenate([x[:rows], jnp.concatenate(side, axis=0)], axis=1)


def place(axis):
    return lax.axis_index(axis).astype(jnp.int32)


def prep_kernel(img_ref, lab_ref, proj_ref, out_ref, part_ref, buf, lab_buf, sem):
    share = part_ref.shape[0]
    at = pl.multiple_of(place("tpl") * share, share)
    copies = start_all(
        [(img_ref, buf), (proj_ref.at[pl.ds(at, share)], part_ref), (lab_ref, lab_buf)], sem
    )
    rows = img_ref.shape[0]
    copies[2].wait()
    lab = lab_buf[...]
    pad = jnp.zeros((14, rows), jnp.int32)
    digits = jnp.concatenate([lab // 128, lab % 128, pad], axis=0)
    out_ref[rows:] = jnp.zeros((16, out_ref.shape[1]), jnp.bfloat16)
    out_ref[rows:, :rows] = digits.astype(jnp.float32).astype(jnp.bfloat16)
    copies[0].wait()
    x = buf[...].astype(jnp.float32)
    out_ref[:rows] = (x * inverse_norm(x)).astype(jnp.bfloat16)
    copies[1].wait()


def lift_kernel(tpl_ref, *rest):
    outs, sem = rest[:-1], rest[-1]
    rows = outs[0].shape[0]
    pairs = [(tpl_ref.at[pl.ds(k * rows, rows)], out) for k, out in enumerate(outs)]
    for copy in start_all(pairs, sem):
        copy.wait()


def tick_kernel(lab_ref, out_ref):
    out_ref[...] = lab_ref[:, :128]


def tick(labels):
    return pl.pallas_call(
        tick_kernel,
        out_shape=sds((1, 128), jnp.int32),
        in_specs=[VM],
        out_specs=VM,
        compiler_params=params(1),
    )(labels)


def join_kernel(n_cls, *rest):
    pieces = rest[:n_cls]
    out_ref, buf, sem = rest[n_cls:]
    copies = start_all([(p, buf.at[place("cls") ^ m]) for m, p in enumerate(pieces)], sem)
    for copy in copies:
        copy.wait()
    width = buf.shape[2]
    for j in range(n_cls):
        out_ref[:, j * width : (j + 1) * width] = buf[j]


def load_projection(places, piece_refs, full_ref, sem):
    me, it = place("img"), place("tpl")
    pairs = [
        (piece, full_ref.at[me ^ m, it ^ t])
        for piece, (m, t) in zip(piece_refs, places)
    ]
    for copy in start_all(pairs, sem):
        copy.wait()


def text_kernel(places, n_tpl, n_half, *rest):
    tpls, rest = rest[:n_half], rest[n_half:]
    n = len(places)
    full_ref, u_ref, rz_ref, sum_ref, send_ref, sem = rest[n:]
    load_projection(places, rest[:n], full_ref, sem)
    feat = tpls[0].shape[1]
    full = full_ref[...].reshape(feat, feat)
    tpl = jnp.concatenate([ref[...] for ref in tpls], axis=0)
    z = jnp.dot(tpl, full, preferred_element_type=jnp.float32)
    rz = inverse_norm(z)
    u = z * rz
    u_ref[...] = u
    rz_ref[...] = rz
    rows = u.shape[0] // n_tpl
    total = u[:rows]
    for t in range(1, n_tpl):
        total = total + u[t * rows : (t + 1) * rows]
    sum_ref[...] = total
    send_ref[...] = total.astype(jnp.bfloat16)


def score_kernel(tpl_total, n_piece, n_other, rows, sum_ref, *rest):
    others = rest[:n_other]
    images = rest[n_other : n_other + n_piece]
    w_ref, rn_ref, e_ref, tot_ref = rest[n_other + n_piece :]
    mean = sum_ref[...]
    for other in others:
        mean = mean + other[...].astype(jnp.float32)
    mean = mean / tpl_total
    rn = inverse_norm(mean)
    w = mean * rn
    w_ref[...] = w
    rn_ref[...] = rn
    wb = w.astype(jnp.bfloat16)
    for k in range(n_piece):
        scores = logit_scale * lax.dot_general(
            wb, images[k][:rows], (((1,), (1,)), ((), ())), preferred_element_type=jnp.float32
        )
        e = jnp.exp(scores)
        e_ref[k] = e
        tot_ref[k : k + 1] = jnp.sum(e, axis=0, keepdims=True)


def fold_totals_kernel(order, tot_ref, *rest):
    others, out_ref = rest[:-1], rest[-1]
    where = {key: k for k, key in enumerate(order)}
    for k, (t, i) in enumerate(order):
        row = tot_ref[k : k + 1]
        for m, other in enumerate(others, 1):
            j = where[t, i ^ m]
            row = row + other[j : j + 1]
        out_ref[k : k + 1] = row


def grad_kernel(tpl_total, n_tpl, n_piece, n_tot, img_rows, n_cls, *rest):
    tots = rest[:n_tot]
    images = rest[n_tot : n_tot + n_piece]
    e_ref, w_ref, rn_ref, u_ref, rz_ref = rest[n_tot + n_piece : n_tot + n_piece + 5]
    outs = rest[n_tot + n_piece + 5 :]
    gz_ref, turned = outs[0], outs[1 : 1 + n_cls]
    flip = outs[1 + n_cls]
    totals = tots[0][...]
    for other in tots[1:]:
        totals = totals + other[...]
    inv = 1.0 / totals
    rows, feat = w_ref.shape
    acc = jnp.zeros((rows, feat), jnp.float32)
    first = (place("cls") * lax.axis_size("img") + place("img")) * rows
    ids = first + lax.broadcasted_iota(jnp.int32, (rows, img_rows), 0)
    for k in range(n_piece):
        digits = images[k][img_rows:, :img_rows].astype(jnp.float32)
        lab = (digits[0:1] * 128.0 + digits[1:2]).astype(jnp.int32)
        hot = (lab == ids).astype(jnp.float32)
        gl = (e_ref[k] * inv[k : k + 1] - hot).astype(jnp.bfloat16)
        acc = acc + jnp.dot(gl, images[k][:img_rows], preferred_element_type=jnp.float32)
    g = logit_scale * acc
    w = w_ref[...]
    dot_wg = jnp.sum(w * g, axis=1, keepdims=True)
    per_u = (g - w * dot_wg) * rn_ref[...] / tpl_total
    inners = []
    for t in range(n_tpl):
        sl = slice(t * rows, (t + 1) * rows)
        u = u_ref[sl]
        inner = jnp.sum(u * per_u, axis=1, keepdims=True)
        gz_ref[sl] = ((per_u - u * inner) * rz_ref[sl]).astype(jnp.bfloat16)
        inners.append(inner)
    line = digits_row(jnp.concatenate(inners, axis=0))
    half = line.shape[1] // 2
    for a in range(feat // 128):
        sl = slice(a * 128, (a + 1) * 128)
        flip[sl] = per_u[:, sl].T
    width = feat // n_cls
    for m, out in enumerate(turned):
        at = (place("cls") ^ m) * width
        top = flip[pl.ds(pl.multiple_of(at, 8), width // 2), :]
        low = flip[pl.ds(pl.multiple_of(at + width // 2, 8), width // 2), :]
        out[: width // 2] = jnp.concatenate([top, low], axis=1).astype(jnp.bfloat16)
        out[width // 2 :] = jnp.concatenate(
            [line[:2, :half], line[:2, half:], jnp.zeros((12, half), jnp.float32)], axis=0
        ).astype(jnp.bfloat16)


def digits_row(column):
    wide = jnp.broadcast_to(column, (column.shape[0], 128)).T
    high = wide[0:1].astype(jnp.bfloat16).astype(jnp.float32)
    return jnp.concatenate([high, wide[0:1] - high], axis=0)


def turn_kernel(n_cls, u_ref, rz_ref, *rest):
    outs, flip = rest[:n_cls], rest[n_cls]
    feat = u_ref.shape[1]
    for a in range(feat // 128):
        sl = slice(a * 128, (a + 1) * 128)
        flip[sl] = u_ref[:, sl].T.astype(jnp.bfloat16)
    line = digits_row(rz_ref[...])
    line = jnp.concatenate([line, jnp.zeros((14, line.shape[1]), jnp.float32)], axis=0)
    width = feat // n_cls
    for m, out in enumerate(outs):
        at = pl.multiple_of((place("cls") ^ m) * width, width)
        out[:width] = flip[pl.ds(at, width), :]
        out[width:] = line.astype(jnp.bfloat16)


def turned_grad(unit_ref, late_ref):
    rows = unit_ref.shape[0] - 16
    unit = unit_ref[:rows].astype(jnp.float32)
    rz = unit_ref[rows:].astype(jnp.float32)
    late = late_ref[: rows // 2].astype(jnp.float32)
    tail = late_ref[rows // 2 :].astype(jnp.float32)
    span = late.shape[1] // 2
    per_u = jnp.concatenate([late[:, :span], late[:, span:]], axis=0)
    per_u = jnp.concatenate([per_u] * (unit.shape[1] // span), axis=1)
    inner = jnp.concatenate([tail[0:1] + tail[1:2], tail[2:3] + tail[3:4]], axis=1)
    return ((per_u - unit * inner) * (rz[0:1] + rz[1:2])).astype(jnp.bfloat16)


def back_kernel(gz_ref, full_ref, *rest):
    out_ref = rest[-1]
    out_ref[...] = lax.dot_general(
        gz_ref[...], full_ref[...], (((1,), (1,)), ((), ())), preferred_element_type=jnp.float32
    ).astype(jnp.bfloat16)


def outer_own_kernel(unit_ref, late_ref, *rest):
    tpl = jnp.concatenate([ref[...] for ref in rest[:-1]], axis=0)
    grad = turned_grad(unit_ref, late_ref)
    rest[-1][...] = jnp.dot(grad, tpl, preferred_element_type=jnp.float32)


def outer_kernel(n_img, n_cls, n_half, held, first_ref, *rest):
    units, lates = rest[: n_cls - 1], rest[n_cls - 1 : 2 * n_cls - 2]
    tpls = rest[2 * n_cls - 2 : -3]
    keep_ref, send_ref, acc_ref = rest[-3:]
    grads = [turned_grad(a, b) for a, b in zip(units, lates)]

    def product(m, slot):
        parts = tpls[slot * n_half : (slot + 1) * n_half]
        tpl = jnp.concatenate([ref[...] for ref in parts], axis=0)
        return jnp.dot(grads[m - 1], tpl, preferred_element_type=jnp.float32)

    first = first_ref[...]
    plans = {}
    for z in range(n_cls):
        plans.setdefault(held(z), []).append(z)
    for plan, spots in plans.items():
        here = functools.reduce(jnp.logical_or, [place("cls") == z for z in spots])

        @pl.when(here)
        def _():
            acc = first
            for m in range(1, n_cls):
                acc = acc + product(m, plan[m - 1])
            acc_ref[...] = acc

    width = acc_ref.shape[1] // n_img
    for j in range(n_img):
        k = place("img") ^ j
        part = pack(acc_ref[:, j * width : (j + 1) * width])

        @pl.when(k % 2 == 0)
        def _():
            keep_ref[k // 2] = part

        @pl.when(k % 2 == 1)
        def _():
            send_ref[k // 2] = part.astype(jnp.bfloat16)


def final_kernel(own_ref, *rest):
    total = own_ref[...]
    for other in rest[:-1]:
        total = total + other[...].astype(jnp.float32)
    cols, rows = rest[-1].shape
    rest[-1][...] = unpack(total, rows, cols).T


def fold_kernel(keep_ref, recv_ref, own_ref, *outs):
    own = keep_ref[0] + recv_ref[0].astype(jnp.float32)
    own_ref[...] = own
    outs[0][...] = own.astype(jnp.bfloat16)
    for k in range(1, len(outs)):
        outs[k][...] = (keep_ref[k] + recv_ref[k].astype(jnp.float32)).astype(jnp.bfloat16)


def both(x, tpl_mask, img_mask):
    if img_mask == 0:
        return swap(x, "tpl", tpl_mask)
    if tpl_mask == 0:
        return swap(x, "img", img_mask)
    n_img, n_tpl = lax.axis_size("img"), lax.axis_size("tpl")
    pairs = [
        (i * n_tpl + t, (i ^ img_mask) * n_tpl + (t ^ tpl_mask))
        for i in range(n_img)
        for t in range(n_tpl)
    ]
    return lax.ppermute(x, ("img", "tpl"), pairs)


def gather_line(parts):
    n = lax.axis_size("cls")
    if n != 4:
        arrays = [[swap(x, "cls", m) for x in parts] for m in range(1, n)]
        return (lambda z: tuple(range(n - 1))), arrays
    one, mid, inner, outer, last = [], [], [], [], []
    for k, x in enumerate(parts):
        one.append(swap(x, "cls", 1))
        mid.append(lax.ppermute(x, "cls", [(1, 2), (2, 1)]))
        inner.append(lax.ppermute(one[k], "cls", [(1, 2), (2, 1)]))
        outer.append(lax.ppermute(mid[k], "cls", [(1, 0), (2, 3)]))
        last.append(lax.ppermute(inner[k], "cls", [(1, 0), (2, 3)]))
    return (lambda z: (0, 2, 1) if z in (1, 2) else (0, 3, 4)), [one, mid, inner, outer, last]


def body(*args):
    return fast_body(*args)


def fast_body(images, labels, templates, projection):
    tpl_count, cls_count, feat = templates.shape
    n_tpl, n_img, n_cls = (lax.axis_size(a) for a in ("tpl", "img", "cls"))
    tpl_total = tpl_count * n_tpl
    flat_rows = tpl_count * cls_count
    img_rows = images.shape[0]
    proj_rows, proj_cols = projection.shape
    f32, bf16 = jnp.float32, jnp.bfloat16
    far = tuple(range(2, n_img, 2))
    tpls = tuple(range(1, n_tpl))
    label_row = labels.reshape(1, img_rows)
    ticks = [tick(label_row) for _ in range(7)]

    share = proj_rows // n_tpl
    marked, part = pl.pallas_call(
        prep_kernel,
        out_shape=(sds((img_rows + 16, feat), bf16), sds((share, proj_cols), bf16)),
        in_specs=[HB, HB, HB],
        out_specs=(VM, VM),
        scratch_shapes=[
            pltpu.VMEM((img_rows, feat), bf16),
            pltpu.VMEM((1, img_rows), jnp.int32),
            pltpu.SemaphoreType.DMA((3,)),
        ],
        compiler_params=params(8),
        name="prep",
    )(*(pltpu.with_memory_space_constraint(x, pltpu.HBM) for x in (images, label_row, projection)))
    shards = [part] + [swap(part, "cls", m) for m in range(1, n_cls)]
    images_at = {(0, 0): marked}
    for m in far:
        images_at[0, m] = swap(marked, "img", m)
    for t in tpls:
        images_at[t, 0] = swap(marked, "tpl", t)

    wide = pl.pallas_call(
        functools.partial(join_kernel, n_cls),
        out_shape=sds((share, feat), bf16),
        in_specs=[HB] * n_cls,
        out_specs=VM,
        scratch_shapes=[
            pltpu.VMEM((n_cls, share, proj_cols), bf16),
            pltpu.SemaphoreType.DMA((n_cls,)),
        ],
        compiler_params=params(4),
        name="join",
    )(*shards)
    proj_at = {(0, 0): wide}
    for m in far:
        proj_at[m, 0] = swap(wide, "img", m)
    for t in tpls:
        proj_at[0, t] = swap(wide, "tpl", t)
    for m in far:
        for t in tpls:
            proj_at[m, t] = swap(proj_at[m, 0], "tpl", t)
    for (m, t), part in list(proj_at.items()):
        proj_at[m ^ 1, t] = swap(part, "img", 1)
    places = list(proj_at)
    proj_list = list(proj_at.values())

    for m in far:
        for t in tpls:
            images_at[t, m] = swap(images_at[t, 0], "img", m)
    for (t, m), piece in list(images_at.items()):
        images_at[t, m ^ 1] = swap(piece, "img", 1)
    order = list(images_at)
    n_piece = len(order)
    image_list = list(images_at.values())

    flat_tpl = templates.reshape(flat_rows, feat)
    near_tpl = pl.pallas_call(
        lift_kernel,
        out_shape=[sds((flat_rows // 2, feat), bf16)] * 2,
        in_specs=[HB],
        out_specs=[VM] * 2,
        scratch_shapes=[pltpu.SemaphoreType.DMA((2,))],
        compiler_params=params(2),
        name="lift",
    )(flat_tpl)
    full, u, rz, local_sum, send_sum = pl.pallas_call(
        functools.partial(text_kernel, places, tpl_count, len(near_tpl)),
        out_shape=(
            sds((n_img, n_tpl, share, feat), bf16),
            sds((flat_rows, feat), f32),
            sds((flat_rows, 1), f32),
            sds((cls_count, feat), f32),
            sds((cls_count, feat), bf16),
        ),
        in_specs=[VM] * len(near_tpl) + [HB] * len(places),
        out_specs=(VM, VM, VM, VM, VM),
        scratch_shapes=[pltpu.SemaphoreType.DMA((len(places),))],
        compiler_params=params(16),
        name="text",
    )(*near_tpl, *proj_list)

    held, tpl_parts = gather_line(near_tpl)
    tpl_list = [x for parts in tpl_parts for x in parts]

    others = [swap(send_sum, "tpl", t) for t in tpls]
    width = feat // n_cls
    units = pl.pallas_call(
        functools.partial(turn_kernel, n_cls),
        out_shape=[sds((width + 16, flat_rows), bf16)] * n_cls,
        in_specs=[VM, VM],
        out_specs=[VM] * n_cls,
        scratch_shapes=[pltpu.VMEM((feat, flat_rows), bf16)],
        compiler_params=params(4),
        name="turn",
    )(u, rz)
    units = [units[0]] + [swap(units[m], "cls", m) for m in range(1, n_cls)]

    class_w, mean_rn, e, tot = pl.pallas_call(
        functools.partial(score_kernel, tpl_total, n_piece, len(others), img_rows),
        out_shape=(
            sds((cls_count, feat), f32),
            sds((cls_count, 1), f32),
            sds((n_piece, cls_count, img_rows), f32),
            sds((n_piece, img_rows), f32),
        ),
        in_specs=[VM] * (1 + len(others) + n_piece),
        out_specs=(VM, VM, VM, VM),
        compiler_params=params(16),
        name="score",
    )(local_sum, *others, *image_list)

    total = pl.pallas_call(
        functools.partial(fold_totals_kernel, order),
        out_shape=sds((n_piece, img_rows), f32),
        in_specs=[VM] * n_img,
        out_specs=VM,
        compiler_params=params(2),
        name="fold_totals",
    )(tot, *[swap(tot, "img", m) for m in range(1, n_img)])
    totals = [total] + [swap(total, "cls", m) for m in range(1, n_cls)]

    gz, *turned = pl.pallas_call(
        functools.partial(
            grad_kernel, tpl_total, tpl_count, n_piece, len(totals), img_rows, n_cls
        ),
        out_shape=[sds((flat_rows, feat), bf16)] + [sds((width // 2 + 16, flat_rows // 2), bf16)] * n_cls,
        in_specs=[VM] * (len(totals) + n_piece + 5),
        out_specs=[VM] * (1 + n_cls),
        scratch_shapes=[pltpu.VMEM((feat, cls_count), f32)],
        compiler_params=params(20),
        name="grad",
    )(
        *totals, *image_list, e, class_w, mean_rn, u, rz,
    )

    lates = [turned[0]] + [swap(turned[m], "cls", m) for m in range(1, n_cls)]
    first = pl.pallas_call(
        outer_own_kernel,
        out_shape=sds((width, feat), f32),
        in_specs=[VM] * (2 + len(near_tpl)),
        out_specs=VM,
        compiler_params=params(8),
        name="outer_own",
    )(units[0], turned[0], *near_tpl)
    grad_tpl = pl.pallas_call(
        back_kernel,
        out_shape=sds((flat_rows, feat), bf16),
        in_specs=[VM] * (2 + len(ticks)),
        out_specs=VM,
        compiler_params=params(16),
        cost_estimate=pl.CostEstimate(
            flops=2 * flat_rows * feat * feat,
            bytes_accessed=2 * feat * feat + 4 * flat_rows * feat,
            transcendentals=0,
        ),
        name="back",
    )(gz, full.reshape(feat, feat), *ticks)

    block = packed_shape(width, feat // n_img)
    keep, send = pl.pallas_call(
        functools.partial(outer_kernel, n_img, n_cls, len(near_tpl), held),
        out_shape=(sds((n_img // 2, *block), f32), sds((n_img // 2, *block), bf16)),
        in_specs=[VM] * (2 * n_cls - 1 + len(tpl_list)),
        out_specs=(VM, VM),
        scratch_shapes=[pltpu.VMEM((width, feat), f32)],
        compiler_params=params(16),
        name="outer",
    )(first, *units[1:], *lates[1:], *tpl_list)
    own, own_b, *far_b = pl.pallas_call(
        fold_kernel,
        out_shape=[sds(block, f32)] + [sds(block, bf16)] * (n_img // 2),
        in_specs=[VM, VM],
        out_specs=[VM] * (1 + n_img // 2),
        compiler_params=params(8),
        name="fold",
    )(keep, swap(send, "img", 1))
    late = [
        both(([own_b] + far_b)[m // 2], t, m)
        for t in range(n_tpl)
        for m in (0, *far)
        if t or m
    ]
    result = pl.pallas_call(
        final_kernel,
        out_shape=sds((feat // n_img, width), f32),
        in_specs=[VM] * (1 + len(late)),
        out_specs=VM,
        compiler_params=params(4),
        name="final",
    )(own, *late)
    return grad_tpl.reshape(tpl_count, cls_count, feat), result


def solution(mesh):
    shape = mesh.shape
    in_specs = (
        P(("img", "tpl"), None),
        P(("img", "tpl")),
        P("tpl", ("cls", "img"), None),
        P("img", "cls"),
    )
    out_specs = (P("tpl", ("cls", "img"), None), P("img", "cls"))

    def step(images, labels, templates, projection):
        powers = all(shape[a] & (shape[a] - 1) == 0 for a in ("img", "cls", "tpl"))
        small = images.size * images.dtype.itemsize <= 8 * MIB
        chosen = body if powers and shape["img"] > 1 and small else general_body
        return jax.shard_map(
            chosen, mesh=mesh, in_specs=in_specs, out_specs=out_specs, check_vma=False
        )(images, labels, templates, projection)

    return step
```

```python
import functools

import jax
import jax.numpy as jnp
from jax import lax
from jax.experimental import pallas as pl
from jax.experimental.pallas import tpu as pltpu
from jax.sharding import PartitionSpec as P


logit_scale = 50.0
epsilon = 1e-06
MIB = 1 << 20
VM = pl.BlockSpec(memory_space=pltpu.VMEM)
HB = pl.BlockSpec(memory_space=pltpu.HBM)


def inverse_norm(values):
    return lax.rsqrt(jnp.sum(values * values, axis=-1, keepdims=True) + epsilon)


def general_body(images, labels, templates, projection):
    tpl_count = templates.shape[0]
    cls_count = templates.shape[1]
    feat_width = templates.shape[2]
    tpl_total = tpl_count * lax.axis_size("tpl")
    img_count = lax.axis_size("img")
    wide_proj = lax.all_gather(projection, "cls", axis=1, tiled=True)
    full_proj = lax.all_gather(wide_proj, "img", axis=0, tiled=True)
    flat_tpl = templates.reshape(tpl_count * cls_count, feat_width)
    text_z = jnp.dot(flat_tpl, full_proj, preferred_element_type=jnp.float32)
    text_rz = inverse_norm(text_z)
    text_u = text_z * text_rz
    u_three = text_u.reshape(tpl_count, cls_count, feat_width)
    local_sum = jnp.sum(u_three, axis=0)
    mean_emb = lax.psum(local_sum, "tpl") / tpl_total
    mean_rn = inverse_norm(mean_emb)
    class_w = mean_emb * mean_rn
    class_b = class_w.astype(jnp.bfloat16)
    img_f = images.astype(jnp.float32)
    img_b = (img_f * inverse_norm(img_f)).astype(jnp.bfloat16)
    class_panel = lax.all_gather(class_b, "img", axis=0, tiled=True)
    scores = logit_scale * jnp.einsum(
        "cd,nd->cn", class_panel, img_b, preferred_element_type=jnp.float32
    )
    exp_scores = jnp.exp(scores)
    totals = lax.psum(jnp.sum(exp_scores, axis=0), "cls")
    first_id = lax.axis_index("cls") * img_count * cls_count
    class_ids = first_id + lax.broadcasted_iota(jnp.int32, (class_panel.shape[0], 1), 0)
    one_hot = (labels[None, :] == class_ids).astype(jnp.float32)
    grad_logit = (exp_scores / totals[None, :] - one_hot).astype(jnp.bfloat16)
    spread = lax.psum_scatter(
        logit_scale * jnp.dot(grad_logit, img_b, preferred_element_type=jnp.float32),
        "img",
        scatter_dimension=0,
        tiled=True,
    )
    class_g = lax.psum(spread, "tpl")
    dot_wg = jnp.sum(class_w * class_g, axis=1, keepdims=True)
    grad_mean = (class_g - class_w * dot_wg) * mean_rn
    per_u = grad_mean / tpl_total
    inner_prod = jnp.sum(u_three * per_u[None], axis=2, keepdims=True)
    grad_z = (
        (per_u[None] - u_three * inner_prod) * text_rz.reshape(tpl_count, cls_count, 1)
    ).astype(jnp.bfloat16)
    grad_flat = grad_z.reshape(tpl_count * cls_count, feat_width)
    grad_tpl = lax.dot_general(
        grad_flat, full_proj, (((1,), (1,)), ((), ())), preferred_element_type=jnp.float32
    )
    grad_templates = grad_tpl.astype(jnp.bfloat16).reshape(tpl_count, cls_count, feat_width)
    tpl_columns = lax.all_to_all(flat_tpl, "img", split_axis=1, concat_axis=0, tiled=True)
    partial_proj = lax.dot_general(
        tpl_columns,
        lax.all_gather(grad_flat, "img", axis=0, tiled=True),
        (((0,), (0,)), ((), ())),
        preferred_element_type=jnp.float32,
    )
    shared_proj = lax.psum_scatter(
        partial_proj.astype(jnp.bfloat16), "cls", scatter_dimension=1, tiled=True
    )
    grad_projection = lax.psum(shared_proj, "tpl").astype(jnp.float32)
    return (grad_templates, grad_projection)


def sds(shape, dtype):
    return jax.ShapeDtypeStruct(shape, dtype)


def swap(x, axis, mask):
    n = lax.axis_size(axis)
    return lax.ppermute(x, axis, [(i, i ^ mask) for i in range(n)])


def params(mib):
    return pltpu.CompilerParams(vmem_limit_bytes=int(mib * MIB))


def start_all(pairs, sem):
    copies = [pltpu.make_async_copy(s, d, sem.at[k]) for k, (s, d) in enumerate(pairs)]
    for copy in copies:
        copy.start()
    return copies


def packing(rows, cols):
    lanes, rest = cols // 128 * 128, cols % 128
    if rest and lanes % rest == 0 and rows % (lanes // rest * 8) == 0:
        return lanes, rest, lanes // rest
    return cols, 0, 0


def packed_shape(rows, cols):
    lanes, rest, pieces = packing(rows, cols)
    return (rows + rows // pieces, lanes) if rest else (rows, cols)


def pack(x):
    rows, cols = x.shape
    lanes, rest, pieces = packing(rows, cols)
    if not rest:
        return x
    step = rows // pieces
    side = [x[q * step : (q + 1) * step, lanes:] for q in range(pieces)]
    return jnp.concatenate([x[:, :lanes], jnp.concatenate(side, axis=1)], axis=0)


def unpack(x, rows, cols):
    _, rest, pieces = packing(rows, cols)
    if not rest:
        return x
    side = [x[rows:, q * rest : (q + 1) * rest] for q in range(pieces)]
    return jnp.concatenate([x[:rows], jnp.concatenate(side, axis=0)], axis=1)


def place(axis):
    return lax.axis_index(axis).astype(jnp.int32)


def prep_kernel(img_ref, lab_ref, proj_ref, out_ref, part_ref, buf, lab_buf, sem):
    share = part_ref.shape[0]
    at = pl.multiple_of(place("tpl") * share, share)
    copies = start_all(
        [(img_ref, buf), (proj_ref.at[pl.ds(at, share)], part_ref), (lab_ref, lab_buf)], sem
    )
    rows = img_ref.shape[0]
    copies[2].wait()
    lab = lab_buf[...]
    pad = jnp.zeros((14, rows), jnp.int32)
    digits = jnp.concatenate([lab // 128, lab % 128, pad], axis=0)
    out_ref[rows:] = jnp.zeros((16, out_ref.shape[1]), jnp.bfloat16)
    out_ref[rows:, :rows] = digits.astype(jnp.float32).astype(jnp.bfloat16)
    copies[0].wait()
    x = buf[...].astype(jnp.float32)
    out_ref[:rows] = (x * inverse_norm(x)).astype(jnp.bfloat16)
    copies[1].wait()


def lift_kernel(tpl_ref, *rest):
    outs, sem = rest[:-1], rest[-1]
    rows = outs[0].shape[0]
    pairs = [(tpl_ref.at[pl.ds(k * rows, rows)], out) for k, out in enumerate(outs)]
    for copy in start_all(pairs, sem):
        copy.wait()


def tick_kernel(lab_ref, out_ref):
    out_ref[...] = jnp.zeros_like(out_ref)


def tick(labels):
    return pl.pallas_call(
        tick_kernel,
        out_shape=sds((1, 128), jnp.int32),
        in_specs=[HB],
        out_specs=VM,
        compiler_params=params(1),
    )(pltpu.with_memory_space_constraint(labels, pltpu.HBM))


def join_kernel(n_cls, *rest):
    pieces = rest[:n_cls]
    out_ref, buf, sem = rest[n_cls:]
    copies = start_all([(p, buf.at[place("cls") ^ m]) for m, p in enumerate(pieces)], sem)
    for copy in copies:
        copy.wait()
    width = buf.shape[2]
    for j in range(n_cls):
        out_ref[:, j * width : (j + 1) * width] = buf[j]


def load_projection(places, piece_refs, full_ref, sem):
    me, it = place("img"), place("tpl")
    pairs = [
        (piece, full_ref.at[me ^ m, it ^ t])
        for piece, (m, t) in zip(piece_refs, places)
    ]
    for copy in start_all(pairs, sem):
        copy.wait()


def text_kernel(places, n_tpl, n_half, *rest):
    tpls, rest = rest[:n_half], rest[n_half:]
    n = len(places)
    full_ref, u_ref, rz_ref, sum_ref, send_ref, sem = rest[n:]
    load_projection(places, rest[:n], full_ref, sem)
    feat = tpls[0].shape[1]
    full = full_ref[...].reshape(feat, feat)
    tpl = jnp.concatenate([ref[...] for ref in tpls], axis=0)
    z = jnp.dot(tpl, full, preferred_element_type=jnp.float32)
    rz = inverse_norm(z)
    u = z * rz
    u_ref[...] = u
    rz_ref[...] = rz
    rows = u.shape[0] // n_tpl
    total = u[:rows]
    for t in range(1, n_tpl):
        total = total + u[t * rows : (t + 1) * rows]
    sum_ref[...] = total
    send_ref[...] = total.astype(jnp.bfloat16)


def score_kernel(tpl_total, n_piece, n_other, rows, sum_ref, *rest):
    others = rest[:n_other]
    images = rest[n_other : n_other + n_piece]
    w_ref, rn_ref, e_ref, tot_ref = rest[n_other + n_piece :]
    mean = sum_ref[...]
    for other in others:
        mean = mean + other[...].astype(jnp.float32)
    mean = mean / tpl_total
    rn = inverse_norm(mean)
    w = mean * rn
    w_ref[...] = w
    rn_ref[...] = rn
    wb = w.astype(jnp.bfloat16)
    for k in range(n_piece):
        scores = logit_scale * lax.dot_general(
            wb, images[k][:rows], (((1,), (1,)), ((), ())), preferred_element_type=jnp.float32
        )
        e = jnp.exp(scores)
        e_ref[k] = e
        tot_ref[k : k + 1] = jnp.sum(e, axis=0, keepdims=True)


def fold_totals_kernel(order, tot_ref, *rest):
    others, out_ref = rest[:-1], rest[-1]
    where = {key: k for k, key in enumerate(order)}
    for k, (t, i) in enumerate(order):
        row = tot_ref[k : k + 1]
        for m, other in enumerate(others, 1):
            j = where[t, i ^ m]
            row = row + other[j : j + 1]
        out_ref[k : k + 1] = row


def grad_kernel(tpl_total, n_tpl, n_piece, n_tot, img_rows, n_cls, *rest):
    tots = rest[:n_tot]
    images = rest[n_tot : n_tot + n_piece]
    e_ref, w_ref, rn_ref, u_ref, rz_ref = rest[n_tot + n_piece : n_tot + n_piece + 5]
    outs = rest[n_tot + n_piece + 5 :]
    gz_ref, turned = outs[0], outs[1 : 1 + n_cls]
    flip = outs[1 + n_cls]
    totals = tots[0][...]
    for other in tots[1:]:
        totals = totals + other[...]
    inv = 1.0 / totals
    rows, feat = w_ref.shape
    acc = jnp.zeros((rows, feat), jnp.float32)
    first = (place("cls") * lax.axis_size("img") + place("img")) * rows
    ids = first + lax.broadcasted_iota(jnp.int32, (rows, img_rows), 0)
    for k in range(n_piece):
        digits = images[k][img_rows:, :img_rows].astype(jnp.float32)
        lab = (digits[0:1] * 128.0 + digits[1:2]).astype(jnp.int32)
        hot = (lab == ids).astype(jnp.float32)
        gl = (e_ref[k] * inv[k : k + 1] - hot).astype(jnp.bfloat16)
        acc = acc + jnp.dot(gl, images[k][:img_rows], preferred_element_type=jnp.float32)
    g = logit_scale * acc
    w = w_ref[...]
    dot_wg = jnp.sum(w * g, axis=1, keepdims=True)
    per_u = (g - w * dot_wg) * rn_ref[...] / tpl_total
    inners = []
    for t in range(n_tpl):
        sl = slice(t * rows, (t + 1) * rows)
        u = u_ref[sl]
        inner = jnp.sum(u * per_u, axis=1, keepdims=True)
        gz_ref[sl] = ((per_u - u * inner) * rz_ref[sl]).astype(jnp.bfloat16)
        inners.append(inner)
    line = digits_row(jnp.concatenate(inners, axis=0))
    half = line.shape[1] // 2
    for a in range(feat // 128):
        sl = slice(a * 128, (a + 1) * 128)
        flip[sl] = per_u[:, sl].T
    width = feat // n_cls
    for m, out in enumerate(turned):
        at = (place("cls") ^ m) * width
        top = flip[pl.ds(pl.multiple_of(at, 8), width // 2), :]
        low = flip[pl.ds(pl.multiple_of(at + width // 2, 8), width // 2), :]
        out[: width // 2] = jnp.concatenate([top, low], axis=1).astype(jnp.bfloat16)
        out[width // 2 :] = jnp.concatenate(
            [line[:2, :half], line[:2, half:], jnp.zeros((12, half), jnp.float32)], axis=0
        ).astype(jnp.bfloat16)


def digits_row(column):
    wide = jnp.broadcast_to(column, (column.shape[0], 128)).T
    high = wide[0:1].astype(jnp.bfloat16).astype(jnp.float32)
    return jnp.concatenate([high, wide[0:1] - high], axis=0)


def turn_kernel(n_cls, u_ref, rz_ref, *rest):
    outs, flip = rest[:n_cls], rest[n_cls]
    feat = u_ref.shape[1]
    for a in range(feat // 128):
        sl = slice(a * 128, (a + 1) * 128)
        flip[sl] = u_ref[:, sl].T.astype(jnp.bfloat16)
    line = digits_row(rz_ref[...])
    line = jnp.concatenate([line, jnp.zeros((14, line.shape[1]), jnp.float32)], axis=0)
    width = feat // n_cls
    for m, out in enumerate(outs):
        at = pl.multiple_of((place("cls") ^ m) * width, width)
        out[:width] = flip[pl.ds(at, width), :]
        out[width:] = line.astype(jnp.bfloat16)


def turned_grad(unit_ref, late_ref):
    rows = unit_ref.shape[0] - 16
    unit = unit_ref[:rows].astype(jnp.float32)
    rz = unit_ref[rows:].astype(jnp.float32)
    late = late_ref[: rows // 2].astype(jnp.float32)
    tail = late_ref[rows // 2 :].astype(jnp.float32)
    span = late.shape[1] // 2
    per_u = jnp.concatenate([late[:, :span], late[:, span:]], axis=0)
    per_u = jnp.concatenate([per_u] * (unit.shape[1] // span), axis=1)
    inner = jnp.concatenate([tail[0:1] + tail[1:2], tail[2:3] + tail[3:4]], axis=1)
    return ((per_u - unit * inner) * (rz[0:1] + rz[1:2])).astype(jnp.bfloat16)


def back_kernel(gz_ref, full_ref, *rest):
    out_ref = rest[-1]
    out_ref[...] = lax.dot_general(
        gz_ref[...], full_ref[...], (((1,), (1,)), ((), ())), preferred_element_type=jnp.float32
    ).astype(jnp.bfloat16)


def outer_own_kernel(unit_ref, late_ref, *rest):
    tpl = jnp.concatenate([ref[...] for ref in rest[:-1]], axis=0)
    grad = turned_grad(unit_ref, late_ref)
    rest[-1][...] = jnp.dot(grad, tpl, preferred_element_type=jnp.float32)


def outer_kernel(n_img, n_cls, n_half, held, first_ref, *rest):
    units, lates = rest[: n_cls - 1], rest[n_cls - 1 : 2 * n_cls - 2]
    tpls = rest[2 * n_cls - 2 : -3]
    keep_ref, send_ref, acc_ref = rest[-3:]
    grads = [turned_grad(a, b) for a, b in zip(units, lates)]

    def product(m, slot):
        parts = tpls[slot * n_half : (slot + 1) * n_half]
        tpl = jnp.concatenate([ref[...] for ref in parts], axis=0)
        return jnp.dot(grads[m - 1], tpl, preferred_element_type=jnp.float32)

    first = first_ref[...]
    plans = {}
    for z in range(n_cls):
        plans.setdefault(held(z), []).append(z)
    for plan, spots in plans.items():
        here = functools.reduce(jnp.logical_or, [place("cls") == z for z in spots])

        @pl.when(here)
        def _():
            acc = first
            for m in range(1, n_cls):
                acc = acc + product(m, plan[m - 1])
            acc_ref[...] = acc

    width = acc_ref.shape[1] // n_img
    for j in range(n_img):
        k = place("img") ^ j
        part = pack(acc_ref[:, j * width : (j + 1) * width])

        @pl.when(k % 2 == 0)
        def _():
            keep_ref[k // 2] = part

        @pl.when(k % 2 == 1)
        def _():
            send_ref[k // 2] = part.astype(jnp.bfloat16)


def final_kernel(own_ref, *rest):
    total = own_ref[...]
    for other in rest[:-1]:
        total = total + other[...].astype(jnp.float32)
    cols, rows = rest[-1].shape
    rest[-1][...] = unpack(total, rows, cols).T


def fold_kernel(keep_ref, recv_ref, own_ref, *outs):
    own = keep_ref[0] + recv_ref[0].astype(jnp.float32)
    own_ref[...] = own
    outs[0][...] = own.astype(jnp.bfloat16)
    for k in range(1, len(outs)):
        outs[k][...] = (keep_ref[k] + recv_ref[k].astype(jnp.float32)).astype(jnp.bfloat16)


def both(x, tpl_mask, img_mask):
    if img_mask == 0:
        return swap(x, "tpl", tpl_mask)
    if tpl_mask == 0:
        return swap(x, "img", img_mask)
    n_img, n_tpl = lax.axis_size("img"), lax.axis_size("tpl")
    pairs = [
        (i * n_tpl + t, (i ^ img_mask) * n_tpl + (t ^ tpl_mask))
        for i in range(n_img)
        for t in range(n_tpl)
    ]
    return lax.ppermute(x, ("img", "tpl"), pairs)


def gather_line(parts):
    n = lax.axis_size("cls")
    if n != 4:
        arrays = [[swap(x, "cls", m) for x in parts] for m in range(1, n)]
        return (lambda z: tuple(range(n - 1))), arrays
    one, mid, inner, outer, last = [], [], [], [], []
    for k, x in enumerate(parts):
        one.append(swap(x, "cls", 1))
        mid.append(lax.ppermute(x, "cls", [(1, 2), (2, 1)]))
        inner.append(lax.ppermute(one[k], "cls", [(1, 2), (2, 1)]))
        outer.append(lax.ppermute(mid[k], "cls", [(1, 0), (2, 3)]))
        last.append(lax.ppermute(inner[k], "cls", [(1, 0), (2, 3)]))
    return (lambda z: (0, 2, 1) if z in (1, 2) else (0, 3, 4)), [one, mid, inner, outer, last]


def body(*args):
    return fast_body(*args)


def fast_body(images, labels, templates, projection):
    tpl_count, cls_count, feat = templates.shape
    n_tpl, n_img, n_cls = (lax.axis_size(a) for a in ("tpl", "img", "cls"))
    tpl_total = tpl_count * n_tpl
    flat_rows = tpl_count * cls_count
    img_rows = images.shape[0]
    proj_rows, proj_cols = projection.shape
    f32, bf16 = jnp.float32, jnp.bfloat16
    far = tuple(range(2, n_img, 2))
    tpls = tuple(range(1, n_tpl))
    label_row = labels.reshape(1, img_rows)
    ticks = [tick(label_row) for _ in range(7)]

    share = proj_rows // n_tpl
    marked, part = pl.pallas_call(
        prep_kernel,
        out_shape=(sds((img_rows + 16, feat), bf16), sds((share, proj_cols), bf16)),
        in_specs=[HB, HB, HB],
        out_specs=(VM, VM),
        scratch_shapes=[
            pltpu.VMEM((img_rows, feat), bf16),
            pltpu.VMEM((1, img_rows), jnp.int32),
            pltpu.SemaphoreType.DMA((3,)),
        ],
        compiler_params=params(8),
        name="prep",
    )(*(pltpu.with_memory_space_constraint(x, pltpu.HBM) for x in (images, label_row, projection)))
    shards = [part] + [swap(part, "cls", m) for m in range(1, n_cls)]
    images_at = {(0, 0): marked}
    for m in far:
        images_at[0, m] = swap(marked, "img", m)
    for t in tpls:
        images_at[t, 0] = swap(marked, "tpl", t)

    wide = pl.pallas_call(
        functools.partial(join_kernel, n_cls),
        out_shape=sds((share, feat), bf16),
        in_specs=[HB] * n_cls,
        out_specs=VM,
        scratch_shapes=[
            pltpu.VMEM((n_cls, share, proj_cols), bf16),
            pltpu.SemaphoreType.DMA((n_cls,)),
        ],
        compiler_params=params(4),
        name="join",
    )(*shards)
    proj_at = {(0, 0): wide}
    for m in far:
        proj_at[m, 0] = swap(wide, "img", m)
    for t in tpls:
        proj_at[0, t] = swap(wide, "tpl", t)
    for m in far:
        for t in tpls:
            proj_at[m, t] = swap(proj_at[m, 0], "tpl", t)
    for (m, t), part in list(proj_at.items()):
        proj_at[m ^ 1, t] = swap(part, "img", 1)
    places = list(proj_at)
    proj_list = list(proj_at.values())

    for m in far:
        for t in tpls:
            images_at[t, m] = swap(images_at[t, 0], "img", m)
    for (t, m), piece in list(images_at.items()):
        images_at[t, m ^ 1] = swap(piece, "img", 1)
    order = list(images_at)
    n_piece = len(order)
    image_list = list(images_at.values())

    flat_tpl = templates.reshape(flat_rows, feat)
    near_tpl = pl.pallas_call(
        lift_kernel,
        out_shape=[sds((flat_rows // 2, feat), bf16)] * 2,
        in_specs=[HB],
        out_specs=[VM] * 2,
        scratch_shapes=[pltpu.SemaphoreType.DMA((2,))],
        compiler_params=params(2),
        name="lift",
    )(pltpu.with_memory_space_constraint(flat_tpl, pltpu.HBM))
    full, u, rz, local_sum, send_sum = pl.pallas_call(
        functools.partial(text_kernel, places, tpl_count, len(near_tpl)),
        out_shape=(
            sds((n_img, n_tpl, share, feat), bf16),
            sds((flat_rows, feat), f32),
            sds((flat_rows, 1), f32),
            sds((cls_count, feat), f32),
            sds((cls_count, feat), bf16),
        ),
        in_specs=[VM] * len(near_tpl) + [HB] * len(places),
        out_specs=(VM, VM, VM, VM, VM),
        scratch_shapes=[pltpu.SemaphoreType.DMA((len(places),))],
        compiler_params=params(16),
        name="text",
    )(*near_tpl, *proj_list)

    held, tpl_parts = gather_line(near_tpl)
    tpl_list = [x for parts in tpl_parts for x in parts]

    others = [swap(send_sum, "tpl", t) for t in tpls]
    width = feat // n_cls
    units = pl.pallas_call(
        functools.partial(turn_kernel, n_cls),
        out_shape=[sds((width + 16, flat_rows), bf16)] * n_cls,
        in_specs=[VM, VM],
        out_specs=[VM] * n_cls,
        scratch_shapes=[pltpu.VMEM((feat, flat_rows), bf16)],
        compiler_params=params(4),
        name="turn",
    )(u, rz)
    units = [units[0]] + [swap(units[m], "cls", m) for m in range(1, n_cls)]

    class_w, mean_rn, e, tot = pl.pallas_call(
        functools.partial(score_kernel, tpl_total, n_piece, len(others), img_rows),
        out_shape=(
            sds((cls_count, feat), f32),
            sds((cls_count, 1), f32),
            sds((n_piece, cls_count, img_rows), f32),
            sds((n_piece, img_rows), f32),
        ),
        in_specs=[VM] * (1 + len(others) + n_piece),
        out_specs=(VM, VM, VM, VM),
        compiler_params=params(16),
        name="score",
    )(local_sum, *others, *image_list)

    total = pl.pallas_call(
        functools.partial(fold_totals_kernel, order),
        out_shape=sds((n_piece, img_rows), f32),
        in_specs=[VM] * n_img,
        out_specs=VM,
        compiler_params=params(2),
        name="fold_totals",
    )(tot, *[swap(tot, "img", m) for m in range(1, n_img)])
    totals = [total] + [swap(total, "cls", m) for m in range(1, n_cls)]

    gz, *turned = pl.pallas_call(
        functools.partial(
            grad_kernel, tpl_total, tpl_count, n_piece, len(totals), img_rows, n_cls
        ),
        out_shape=[sds((flat_rows, feat), bf16)] + [sds((width // 2 + 16, flat_rows // 2), bf16)] * n_cls,
        in_specs=[VM] * (len(totals) + n_piece + 5),
        out_specs=[VM] * (1 + n_cls),
        scratch_shapes=[pltpu.VMEM((feat, cls_count), f32)],
        compiler_params=params(20),
        name="grad",
    )(
        *totals, *image_list, e, class_w, mean_rn, u, rz,
    )

    lates = [turned[0]] + [swap(turned[m], "cls", m) for m in range(1, n_cls)]
    first = pl.pallas_call(
        outer_own_kernel,
        out_shape=sds((width, feat), f32),
        in_specs=[VM] * (2 + len(near_tpl)),
        out_specs=VM,
        compiler_params=params(8),
        name="outer_own",
    )(units[0], turned[0], *near_tpl)
    grad_tpl = pl.pallas_call(
        back_kernel,
        out_shape=sds((flat_rows, feat), bf16),
        in_specs=[VM] * (2 + len(ticks)),
        out_specs=VM,
        compiler_params=params(16),
        cost_estimate=pl.CostEstimate(
            flops=2 * flat_rows * feat * feat,
            bytes_accessed=2 * feat * feat + 4 * flat_rows * feat,
            transcendentals=0,
        ),
        name="back",
    )(gz, full.reshape(feat, feat), *ticks)

    block = packed_shape(width, feat // n_img)
    keep, send = pl.pallas_call(
        functools.partial(outer_kernel, n_img, n_cls, len(near_tpl), held),
        out_shape=(sds((n_img // 2, *block), f32), sds((n_img // 2, *block), bf16)),
        in_specs=[VM] * (2 * n_cls - 1 + len(tpl_list)),
        out_specs=(VM, VM),
        scratch_shapes=[pltpu.VMEM((width, feat), f32)],
        compiler_params=params(16),
        name="outer",
    )(first, *units[1:], *lates[1:], *tpl_list)
    own, own_b, *far_b = pl.pallas_call(
        fold_kernel,
        out_shape=[sds(block, f32)] + [sds(block, bf16)] * (n_img // 2),
        in_specs=[VM, VM],
        out_specs=[VM] * (1 + n_img // 2),
        compiler_params=params(8),
        name="fold",
    )(keep, swap(send, "img", 1))
    late = [
        both(([own_b] + far_b)[m // 2], t, m)
        for t in range(n_tpl)
        for m in (0, *far)
        if t or m
    ]
    result = pl.pallas_call(
        final_kernel,
        out_shape=sds((feat // n_img, width), f32),
        in_specs=[VM] * (1 + len(late)),
        out_specs=VM,
        compiler_params=params(4),
        name="final",
    )(own, *late)
    return grad_tpl.reshape(tpl_count, cls_count, feat), result


def solution(mesh):
    shape = mesh.shape
    in_specs = (
        P(("img", "tpl"), None),
        P(("img", "tpl")),
        P("tpl", ("cls", "img"), None),
        P("img", "cls"),
    )
    out_specs = (P("tpl", ("cls", "img"), None), P("img", "cls"))

    def step(images, labels, templates, projection):
        powers = all(shape[a] & (shape[a] - 1) == 0 for a in ("img", "cls", "tpl"))
        small = images.size * images.dtype.itemsize <= 8 * MIB
        chosen = body if powers and shape["img"] > 1 and small else general_body
        return jax.shard_map(
            chosen, mesh=mesh, in_specs=in_specs, out_specs=out_specs, check_vma=False
        )(images, labels, templates, projection)

    return step
```
